32 devices in a mesh: grp: 16 (over z, x, core), tile: 2 (over y).
Axes of the slice: x: 2, y: 2, z: 4, core: 2. Of those that a mesh axis runs over, the one named last changes fastest.
Arguments:
- spectrum: float32 [1152, 64, 256], P(None, 'tile', 'grp'), may hold values from 0.05 to 2
- matrices: bfloat16 [2, 16, 2, 1152, 1152], P('tile', 'grp'), may hold values from -0.1875 to 0.1875
- ownership: int32 [64, 256], P('tile', 'grp'), may hold values from 0 to 1
- land_mask: int32 [64, 256], P('tile', 'grp'), may hold values 0 or 1
- courant: float32 [2, 1152], replicated, may hold values from -0.45 to 0.45
- stokes_weight: bfloat16 [1152, 256], replicated, may hold values from -0.1875 to 0.1875
- ocean: float32 [4, 64, 256, 128], P(None, 'tile', 'grp'), may hold values from -6 to 6
Outputs:
- spectrum_out: float32 [1152, 64, 256], P(None, 'tile', 'grp')
- ocean_out: float32 [4, 64, 256, 128], P(None, 'tile', 'grp')
The draws below stay inside these ranges and needn't reach their ends.
All inputs are finite; a program needn't handle non-finite values. No bound on the sum of `land_mask` on one device may be relied on, other than what follows from the above.
Results may differ from the reference program's by a relative error of at most 0.0021.
Values sent between devices are 32-bit elements; how exact they have to be, the bound alone decides.
No kernel may reach another device: no remote copies, remote signals or barrier semaphores. Data moves between devices by JAX's collectives and lax.ppermute only.
A program may use at most 128 MiB of HBM per device.

```python
import math
import jax
import jax.numpy as jnp
from jax import lax

BINS = 1152
LEVELS = 128
MATS = 2
STEPS = 2
ROWS_DEV = 32
COLS_DEV = 16
NR = 64
NC = 256
N_GRP = 16
N_TILE = 2


def plant(values, key, least, top_value):
    longest = values.shape.index(max(values.shape))
    spots = []
    for shift in (0, 1):
        where = [jax.random.randint(jax.random.fold_in(key, axis), (), 0, length) for axis, length in enumerate(values.shape)]
        where[longest] = (where[longest] + shift) % values.shape[longest]
        spots.append(tuple(where))
    return values.at[spots[0]].set(least).at[spots[1]].set(top_value)


def block_levels(key, shape, shards, low, top_value):
    def one(position, parts):
        draws = jax.random.uniform(jax.random.fold_in(jax.random.fold_in(key, 6), position), (parts,), jnp.float32, low / len(shards), top_value / len(shards))
        return jnp.repeat(jnp.exp(draws), shape[position] // parts).reshape((-1,) + (1,) * (len(shape) - position - 1))

    level = one(*shards[0])
    for cut in shards[1:]:
        level = level * one(*cut)
    return level


def bell_draw(rng, extent, spread, bound, cuts=(), held_as=jnp.bfloat16):
    result = spread * jax.random.normal(rng, extent, jnp.float32)
    if cuts:
        result = result * block_levels(rng, extent, cuts, -0.22, 0.18)
    return jnp.clip(result, -bound, bound).astype(held_as)


def setup_inputs(seed: int = 0) -> dict:
    splits = jax.random.split(jax.random.key(seed), 8)
    return {
        "spectrum": jnp.clip(jnp.exp(math.log(2.0) - 3.6888794 * jax.random.uniform(splits[0], (BINS, NR, NC), jnp.float32) ** block_levels(splits[0], (BINS, NR, NC), ((1, 2), (2, 16)), -0.2, 0.2)), 0.05, 2.0),
        "matrices": bell_draw(splits[1], (N_TILE, N_GRP, MATS, BINS, BINS), BINS ** -0.5, 0.1875, ((0, 2), (1, 16))),
        "ownership": plant(jax.random.randint(splits[2], (NR, NC), 0, MATS), jax.random.fold_in(splits[2], 1), 0, MATS - 1).astype(jnp.int32),
        "land_mask": plant((jax.random.randint(splits[3], (NR, NC), 0, 10) < 9).astype(jnp.int32), jax.random.fold_in(splits[3], 1), 0, 1),
        "courant": jnp.clip(jax.random.uniform(splits[4], (2, BINS), jnp.float32, -0.45, 0.45), -0.45, 0.45),
        "stokes_weight": bell_draw(splits[5], (BINS, 2 * LEVELS), BINS ** -0.5, 0.1875),
        "ocean": bell_draw(splits[6], (4, NR, NC, LEVELS), 1.0, 6.0, ((1, 2), (2, 16)), jnp.float32),
    }


current_gain = 0.2
source_gain = 0.5
mixing_side = 0.15
mixing_depth = 0.2
rotation = 0.3
transport = 0.5


def upwind(padded, speed_x, speed_y, sea_mask):
    middle = padded[:, 1:-1, 1:-1]
    western = padded[:, 1:-1, :-2]
    eastern = padded[:, 1:-1, 2:]
    northern = padded[:, :-2, 1:-1]
    southern = padded[:, 2:, 1:-1]
    flux = jnp.maximum(speed_x, 0.0) * (middle - western) + jnp.minimum(speed_x, 0.0) * (eastern - middle)
    flux = flux + jnp.maximum(speed_y, 0.0) * (middle - northern) + jnp.minimum(speed_y, 0.0) * (southern - middle)
    return sea_mask[None] * (middle - flux)


def ocean_step(fields, padded, drift, sea_mask):
    northern = padded[:, :-2, 1:-1]
    southern = padded[:, 2:, 1:-1]
    western = padded[:, 1:-1, :-2]
    eastern = padded[:, 1:-1, 2:]
    lateral = northern + southern + western + eastern - 4.0 * fields
    column = jnp.pad(fields, ((0, 0), (0, 0), (0, 0), (1, 1)))
    vertical = column[..., 2:] + column[..., :-2] - 2.0 * fields
    mixing = mixing_side * lateral + mixing_depth * vertical
    tend_u = mixing[0] + rotation * (fields[1] + drift[1])
    tend_v = mixing[1] - rotation * (fields[0] + drift[0])
    grad_x = 0.5 * (eastern[2:] - western[2:])
    grad_y = 0.5 * (southern[2:] - northern[2:])
    tend_tracer = mixing[2:] - transport * (drift[0][None] * grad_x + drift[1][None] * grad_y)
    tendency = jnp.concatenate([tend_u[None], tend_v[None], tend_tracer], 0)
    return fields + sea_mask[None, :, :, None] * tendency


def reference(spectrum, matrices, ownership, land_mask, courant, stokes_weight, ocean):
    sea_mask = land_mask.astype(jnp.float32)
    blocks_count = N_TILE * N_GRP
    points = ROWS_DEV * COLS_DEV
    matrix_set = matrices.reshape(blocks_count, MATS, BINS, BINS)
    owner_blocks = ownership.reshape(N_TILE, ROWS_DEV, N_GRP, COLS_DEV).transpose(0, 2, 1, 3).reshape(blocks_count, 1, 1, points)
    choices_range = jnp.arange(MATS, dtype=jnp.int32)[:, None, None]
    profile = stokes_weight.astype(jnp.float32).reshape(BINS, 2, LEVELS)
    energy = spectrum
    fields = ocean
    for step in range(STEPS):
        current = fields[0:2, :, :, 0]
        speed_x = courant[0][:, None, None] + current_gain * current[0][None]
        speed_y = courant[1][:, None, None] + current_gain * current[1][None]
        padded = jnp.pad(energy, ((0, 0), (1, 1), (1, 1)))
        advected = upwind(padded, speed_x, speed_y, sea_mask)
        low = advected.astype(jnp.bfloat16)
        low_blocks = low.reshape(BINS, N_TILE, ROWS_DEV, N_GRP, COLS_DEV).transpose(1, 3, 0, 2, 4).reshape(blocks_count, BINS, points)

        def apply_block(items):
            matrix_pair, block, owner = items
            products = jnp.einsum("mab,bp->map", matrix_pair.astype(jnp.float32), block.astype(jnp.float32))
            select = (owner[0] == choices_range).astype(jnp.float32)
            return jnp.sum(select * products, axis=0)

        source_blocks = lax.map(apply_block, (matrix_set, low_blocks, owner_blocks))
        source = source_blocks.reshape(N_TILE, N_GRP, BINS, ROWS_DEV, COLS_DEV).transpose(2, 0, 3, 1, 4).reshape(BINS, NR, NC)
        energy = sea_mask[None] * (advected + source_gain * source)
        drift = jnp.einsum("brc,bkl->krcl", energy.astype(jnp.bfloat16).astype(jnp.float32), profile)
        padded_ocean = jnp.pad(fields, ((0, 0), (1, 1), (1, 1), (0, 0)))
        fields = ocean_step(fields, padded_ocean, drift, sea_mask)
    return energy, fields
```

```python
import functools

import jax
import jax.numpy as jnp
from jax import lax
from jax.experimental import pallas as pl
from jax.experimental.pallas import tpu as pltpu
from jax.sharding import PartitionSpec as P

STEPS = 2

current_gain = 0.2
source_gain = 0.5
mixing_side = 0.15
mixing_depth = 0.2
rotation = 0.3
transport = 0.5

LANES = 128
VMEM = pltpu.VMEM
F32 = jnp.float32
BF16 = jnp.bfloat16


def lane_chunks(width):
    return range(0, width, LANES)


def spread(columns, r, cols):
    return jnp.broadcast_to(columns[:, r : r + 1], (cols, LANES))


def pick(flag, yes, no):
    return jnp.where(flag, yes, no)


def pack_borders(dims, e_ref, o_ref, odd_col, odd_row, col_refs, row_refs):
    rows, cols, bins, levels, fields = dims
    points = rows * cols

    def column(c, to_ref):
        start = cols + c
        for k in lane_chunks(bins):
            to_ref[:, k : k + LANES] = e_ref[k // LANES, pl.ds(start, rows, stride=cols), :]
        for q in range(fields):
            to_ref[:, bins + q * levels : bins + (q + 1) * levels] = o_ref[
                q, pl.ds(start, rows, stride=cols), :
            ]

    def row(r, to_ref):
        start = pl.multiple_of(cols + r * cols, cols)
        for k in lane_chunks(bins):
            to_ref[:, k : k + LANES] = e_ref[k // LANES, pl.ds(start, cols), :]
        for q in range(fields):
            to_ref[:, bins + q * levels : bins + (q + 1) * levels] = o_ref[q, pl.ds(start, cols), :]

    for index, to_ref in enumerate(col_refs):
        near = odd_col if index == 0 else 1 - odd_col
        column((cols - 1) * (1 - near), to_ref)
    for index, to_ref in enumerate(row_refs):
        near = odd_row if index == 0 else 1 - odd_row
        row((rows - 1) * (1 - near), to_ref)


def clear_ends(dims, e_ref, o_ref):
    rows, cols, bins, levels, fields = dims
    points = rows * cols
    for start in (0, cols + points):
        for k in range(bins // LANES):
            e_ref[k, start : start + cols, :] = jnp.zeros((cols, LANES), F32)
        for q in range(fields):
            o_ref[q, start : start + cols, :] = jnp.zeros((cols, levels), F32)


def first_kernel(dims, n_col, n_row, parity_ref, e_hbm, o_hbm, *refs):
    rows, cols, bins, levels, fields = dims
    points = rows * cols
    e_ref, o_ref = refs[:2]
    col_refs = refs[2 : 2 + n_col]
    row_refs = refs[2 + n_col : 2 + n_col + n_row]
    sems = refs[-1]
    copies = []
    for k in range(bins // LANES):
        copies.append(
            pltpu.make_async_copy(
                e_hbm.at[:, pl.ds(k * LANES, LANES)],
                e_ref.at[k, pl.ds(cols, points), :],
                sems.at[k],
            )
        )
    for q in range(fields):
        copies.append(
            pltpu.make_async_copy(
                o_hbm.at[q], o_ref.at[q, pl.ds(cols, points), :], sems.at[bins // LANES + q]
            )
        )
    for copy in copies:
        copy.start()
    clear_ends(dims, e_ref, o_ref)
    for copy in copies:
        copy.wait()
    pack_borders(dims, e_ref, o_ref, parity_ref[0], parity_ref[1], col_refs, row_refs)


def advect_rows(dims, e_ref, o_ref, mask_ref, courant_ref, adv_ref):
    rows, cols, bins, levels, fields = dims
    col_id = lax.broadcasted_iota(jnp.int32, (cols, LANES), 0)
    west_end = col_id == 0
    east_end = col_id == cols - 1

    def body(r, _):
        at = pl.multiple_of(r * cols, cols)
        here = pl.multiple_of(cols + r * cols, cols)
        after = pl.multiple_of(2 * cols + r * cols, cols)
        sea = mask_ref[pl.ds(at, cols), :]
        drift_x = jnp.broadcast_to(current_gain * o_ref[0, pl.ds(here, cols), 0:1], (cols, LANES))
        drift_y = jnp.broadcast_to(current_gain * o_ref[1, pl.ds(here, cols), 0:1], (cols, LANES))
        for k in lane_chunks(bins):
            lanes = slice(k, k + LANES)
            mid = e_ref[k // LANES, pl.ds(here, cols), :]
            north = e_ref[k // LANES, pl.ds(at, cols), :]
            south = e_ref[k // LANES, pl.ds(after, cols), :]
            west = jnp.where(west_end, 0.0, pltpu.roll(mid, 1, axis=0))
            east = jnp.where(east_end, 0.0, pltpu.roll(mid, cols - 1, axis=0))
            speed_x = courant_ref[0:1, lanes] + drift_x
            speed_y = courant_ref[1:2, lanes] + drift_y
            flux = speed_x * jnp.where(speed_x > 0, mid - west, east - mid)
            flux = flux + speed_y * jnp.where(speed_y > 0, mid - north, south - mid)
            adv_ref[k // LANES, pl.ds(at, cols), :] = sea * (mid - flux)
        return 0

    lax.fori_loop(0, rows, body, 0)


def advect_first_kernel(
    dims, e_ref, o_ref, mask_t, owner_t, courant_ref, m_hbm, w_hbm,
    adv_ref, mask_ref, owner_ref, m_ref, w_ref, sems,
):
    rows, cols, bins, levels, fields = dims
    copies = [
        pltpu.make_async_copy(m_hbm, m_ref, sems.at[0]),
        pltpu.make_async_copy(w_hbm, w_ref, sems.at[1]),
    ]
    for copy in copies:
        copy.start()
    mask = mask_t[...].astype(F32)
    owner = owner_t[...]
    for r in range(rows):
        mask_ref[r * cols : (r + 1) * cols, :] = spread(mask, r, cols)
        owner_ref[r * cols : (r + 1) * cols, :] = spread(owner, r, cols)
    advect_rows(dims, e_ref, o_ref, mask_ref, courant_ref, adv_ref)
    for copy in copies:
        copy.wait()


def advect_kernel(dims, e_ref, o_ref, mask_ref, courant_ref, adv_ref):
    advect_rows(dims, e_ref, o_ref, mask_ref, courant_ref, adv_ref)


def fix_borders(dims, west, east, north, south, o_ref, mask_ref, courant_ref, adv_ref):
    rows, cols, bins, levels, fields = dims
    points = rows * cols

    def column(c, halo, sign):
        sea = mask_ref[pl.ds(c, rows, stride=cols), :]
        speed = o_ref[0, pl.ds(cols + c, rows, stride=cols), :]
        speed = jnp.broadcast_to(current_gain * speed[:, 0:1], (rows, LANES))
        for k in lane_chunks(bins):
            lanes = slice(k, k + LANES)
            flow = jnp.maximum(sign * (courant_ref[0:1, lanes] + speed), 0.0)
            spots = pl.ds(c, rows, stride=cols)
            adv_ref[k // LANES, spots, :] = (
                adv_ref[k // LANES, spots, :] + sea * flow * halo(lanes)
            )

    def row(r, halo, sign):
        sea = mask_ref[r * cols : (r + 1) * cols, :]
        speed = o_ref[1, cols + r * cols : 2 * cols + r * cols, 0:1]
        speed = jnp.broadcast_to(current_gain * speed, (cols, LANES))
        for k in lane_chunks(bins):
            lanes = slice(k, k + LANES)
            flow = jnp.maximum(sign * (courant_ref[1:2, lanes] + speed), 0.0)
            spots = slice(r * cols, (r + 1) * cols)
            adv_ref[k // LANES, spots, :] = (
                adv_ref[k // LANES, spots, :] + sea * flow * halo(lanes)
            )

    column(0, west, 1.0)
    column(cols - 1, east, -1.0)
    row(0, north, 1.0)
    row(rows - 1, south, -1.0)


def ocean_rows(dims, o_ref, mask_ref, drift_ref, out_ref, out_at):
    rows, cols, bins, levels, fields = dims
    col_id = lax.broadcasted_iota(jnp.int32, (cols, levels), 0)
    west_end = col_id == 0
    east_end = col_id == cols - 1
    level_id = lax.broadcasted_iota(jnp.int32, (cols, levels), 1)
    top = level_id == 0
    bottom = level_id == levels - 1

    def body(r, _):
        at = pl.multiple_of(r * cols, cols)
        here = pl.multiple_of(cols + r * cols, cols)
        after = pl.multiple_of(2 * cols + r * cols, cols)
        sea = mask_ref[pl.ds(at, cols), :]
        drift = [drift_ref[k, pl.ds(at, cols), :] for k in range(2)]
        mid = [o_ref[q, pl.ds(here, cols), :] for q in range(fields)]
        for q in range(fields):
            own = mid[q]
            at_north = o_ref[q, pl.ds(at, cols), :]
            at_south = o_ref[q, pl.ds(after, cols), :]
            at_west = jnp.where(west_end, 0.0, pltpu.roll(own, 1, axis=0))
            at_east = jnp.where(east_end, 0.0, pltpu.roll(own, cols - 1, axis=0))
            above = jnp.where(top, 0.0, pltpu.roll(own, 1, axis=1))
            below = jnp.where(bottom, 0.0, pltpu.roll(own, levels - 1, axis=1))
            lateral = at_north + at_south + at_west + at_east - 4.0 * own
            mixing = mixing_side * lateral + mixing_depth * (below + above - 2.0 * own)
            if q == 0:
                tend = mixing + rotation * (mid[1] + drift[1])
            elif q == 1:
                tend = mixing - rotation * (mid[0] + drift[0])
            else:
                grad = drift[0] * (at_east - at_west) + drift[1] * (at_south - at_north)
                tend = mixing - (0.5 * transport) * grad
            out_ref[q, pl.ds(pl.multiple_of(out_at + r * cols, cols), cols), :] = own + sea * tend
        return 0

    lax.fori_loop(0, rows, body, 0)


def ocean_borders(dims, west, east, north, south, mask_ref, drift_ref, out_ref, out_at):
    rows, cols, bins, levels, fields = dims

    def border(start, count, stride, halo, along, sign):
        def spots(base):
            return pl.ds(base + start, count, stride=stride)

        sea = mask_ref[spots(0), :]
        shear = (sign * 0.5 * transport) * drift_ref[along, spots(0), :]
        for q in range(fields):
            value = halo(slice(bins + q * levels, bins + (q + 1) * levels))
            gain = mixing_side if q < 2 else mixing_side + shear
            out_ref[q, spots(out_at), :] = out_ref[q, spots(out_at), :] + sea * (gain * value)

    border(0, rows, cols, west, 0, 1.0)
    border(cols - 1, rows, cols, east, 0, -1.0)
    border(0, cols, 1, north, 1, 1.0)
    border((rows - 1) * cols, cols, 1, south, 1, -1.0)


def step_kernel(dims, mats, n_col, n_row, last, parity_ref, adv_old, o_in, mask_ref, owner_ref,
                courant_ref, m_ref, w_ref, *refs):
    rows, cols, bins, levels, fields = dims
    points = rows * cols
    got_col = refs[:n_col]
    got_row = refs[n_col : n_col + n_row]
    adv_in, *rest = refs[n_col + n_row :]
    if last:
        e_hbm, o_hbm, low_ref, drift_ref, e_ref, o_ref, sems = rest
    else:
        e_ref, o_ref = rest[:2]
        col_refs = rest[2 : 2 + n_col]
        row_refs = rest[2 + n_col : 2 + n_col + n_row]
        low_ref, drift_ref = rest[2 + n_col + n_row :]
    pad = 0 if last else cols
    odd_col = parity_ref[0] == 1
    odd_row = parity_ref[1] == 1

    def halo(got, odd, before):
        first = got[0]
        second = got[1] if len(got) > 1 else None

        def read(lanes):
            def take(ref):
                return 0.0 if ref is None else ref[:, lanes]

            if before:
                return jnp.where(odd, take(first), take(second))
            return jnp.where(odd, take(second), take(first))

        return read

    west = halo(got_col, odd_col, True)
    east = halo(got_col, odd_col, False)
    north = halo(got_row, odd_row, True)
    south = halo(got_row, odd_row, False)

    fix_borders(dims, west, east, north, south, o_in, mask_ref, courant_ref, adv_in)

    def mask_low(r, _):
        at = pl.multiple_of(r * cols, cols)
        owner = owner_ref[pl.ds(at, cols), :]
        for k in lane_chunks(bins):
            value = adv_in[k // LANES, pl.ds(at, cols), :]
            for m in range(mats):
                low_ref[pl.ds(at, cols), m * bins + k : m * bins + k + LANES] = jnp.where(
                    owner == m, value, 0.0
                ).astype(BF16)
        return 0

    lax.fori_loop(0, rows, mask_low, 0)
    weights = jnp.concatenate([m_ref[m] for m in range(mats)], axis=1)
    source = lax.dot_general(
        low_ref[...], weights, (((1,), (1,)), ((), ())), preferred_element_type=F32
    )
    for k in lane_chunks(bins):
        lanes = slice(k, k + LANES)
        for r in range(rows):
            at = slice(r * cols, (r + 1) * cols)
            energy = mask_ref[at, :] * (adv_in[k // LANES, at, :] + source_gain * source[at, lanes])
            if last:
                e_ref[at, lanes] = energy
            else:
                e_ref[k // LANES, cols + r * cols : 2 * cols + r * cols, :] = energy
            low_ref[at, lanes] = energy.astype(BF16)
    if last:
        e_copy = pltpu.make_async_copy(e_ref, e_hbm, sems.at[0])
        e_copy.start()
    drift = jnp.dot(low_ref[:, 0:bins], w_ref[...], preferred_element_type=F32)
    for k in range(2):
        drift_ref[k] = drift[:, k * levels : (k + 1) * levels]
    ocean_rows(dims, o_in, mask_ref, drift_ref, o_ref, pad)
    ocean_borders(dims, west, east, north, south, mask_ref, drift_ref, o_ref, pad)
    if last:
        o_copy = pltpu.make_async_copy(o_ref, o_hbm, sems.at[1])
        o_copy.start()
        e_copy.wait()
        o_copy.wait()
    else:
        clear_ends(dims, e_ref, o_ref)
        pack_borders(dims, e_ref, o_ref, parity_ref[0], parity_ref[1], col_refs, row_refs)


def swap_pairs(values, axis):
    count = lax.axis_size(axis)
    got = []
    for index, value in enumerate(values):
        pairs = []
        for i in range(index, count - 1, 2):
            pairs += [(i, i + 1), (i + 1, i)]
        got.append(lax.ppermute(value, axis, pairs))
    return got


def local(spectrum, matrices, ownership, land_mask, courant, stokes_weight, ocean):
    bins, rows, cols = spectrum.shape
    fields, _, _, levels = ocean.shape
    mats = matrices.shape[2]
    points = rows * cols
    dims = (rows, cols, bins, levels, fields)
    n_col = 2 if lax.axis_size("grp") > 2 else 1
    n_row = 2 if lax.axis_size("tile") > 2 else 1
    e0 = jnp.transpose(spectrum, (1, 2, 0)).reshape(points, bins)
    o0 = ocean.reshape(fields, points, levels)
    m0 = matrices.reshape(mats, bins, bins)
    mask_t = land_mask.T
    owner_t = ownership.T
    parity = jnp.stack([lax.axis_index("grp") % 2, lax.axis_index("tile") % 2]).astype(jnp.int32)

    vmem = pl.BlockSpec(memory_space=VMEM)
    smem = pl.BlockSpec(memory_space=pltpu.SMEM)
    anys = pl.BlockSpec(memory_space=pl.ANY)
    chunks = bins // LANES
    e_pad = VMEM((chunks, points + 2 * cols, LANES), F32)
    o_pad = VMEM((fields, points + 2 * cols, levels), F32)
    wide = bins + fields * levels
    borders = [VMEM((rows, wide), F32)] * n_col + [VMEM((cols, wide), F32)] * n_row
    n_all = n_col + n_row

    def params(mib):
        return pltpu.CompilerParams(vmem_limit_bytes=mib * 2**20)

    def exchange(sent):
        return swap_pairs(sent[:n_col], "grp") + swap_pairs(sent[n_col:], "tile")

    e, o, *sent = pl.pallas_call(
        functools.partial(first_kernel, dims, n_col, n_row),
        out_shape=[e_pad, o_pad] + borders,
        in_specs=[smem, anys, anys],
        out_specs=[vmem] * (2 + n_all),
        scratch_shapes=[pltpu.SemaphoreType.DMA((chunks + fields,))],
        compiler_params=params(8),
        name="first",
    )(parity, e0, o0)
    got = exchange(sent)
    adv, mask, owner, m, w = pl.pallas_call(
        functools.partial(advect_first_kernel, dims),
        out_shape=[
            VMEM((chunks, points, LANES), F32),
            VMEM((points, LANES), F32),
            VMEM((points, LANES), jnp.int32),
            VMEM((mats, bins, bins), BF16),
            VMEM(stokes_weight.shape, BF16),
        ],
        in_specs=[vmem] * 5 + [anys] * 2,
        out_specs=[vmem] * 5,
        scratch_shapes=[pltpu.SemaphoreType.DMA((2,))],
        compiler_params=params(16),
        name="advect_first",
    )(e, o, mask_t, owner_t, courant, m0, stokes_weight)
    for step in range(STEPS):
        last = step == STEPS - 1
        scratch = [VMEM((points, mats * bins), BF16), VMEM((2, points, levels), F32)]
        if last:
            out_shape = [
                jax.ShapeDtypeStruct((points, bins), F32),
                jax.ShapeDtypeStruct((fields, points, levels), F32),
            ]
            out_specs = [anys, anys]
            scratch += [
                VMEM((points, bins), F32),
                VMEM((fields, points, levels), F32),
                pltpu.SemaphoreType.DMA((2,)),
            ]
        else:
            out_shape = [e_pad, o_pad] + borders
            out_specs = [vmem] * (2 + n_all)
        out = pl.pallas_call(
            functools.partial(step_kernel, dims, mats, n_col, n_row, last),
            out_shape=[VMEM(adv.shape, F32)] + out_shape,
            in_specs=[smem] + [vmem] * (7 + n_all),
            out_specs=[vmem] + out_specs,
            input_output_aliases={1: 0},
            scratch_shapes=scratch,
            compiler_params=params(40),
            name="step_last" if last else "step",
        )(parity, adv, o, mask, owner, courant, m, w, *got)
        if last:
            _, energy, fields_out = out
        else:
            _, e, o, *sent = out
            got = exchange(sent)
            adv = pl.pallas_call(
                functools.partial(advect_kernel, dims),
                out_shape=VMEM((chunks, points, LANES), F32),
                in_specs=[vmem] * 4,
                out_specs=vmem,
                compiler_params=params(16),
                name="advect",
            )(e, o, mask, courant)
    energy = jnp.transpose(energy.reshape(rows, cols, bins), (2, 0, 1))
    return energy, fields_out.reshape(ocean.shape)


def solution(mesh):
    in_specs = (
        P(None, "tile", "grp"),
        P("tile", "grp", None, None, None),
        P("tile", "grp"),
        P("tile", "grp"),
        P(),
        P(),
        P(None, "tile", "grp", None),
    )
    out_specs = (P(None, "tile", "grp"), P(None, "tile", "grp", None))
    return jax.shard_map(local, mesh=mesh, in_specs=in_specs, out_specs=out_specs, check_vma=False)
```

```python
import functools

import jax
import jax.numpy as jnp
from jax import lax
from jax.experimental import pallas as pl
from jax.experimental.pallas import tpu as pltpu
from jax.sharding import PartitionSpec as P

STEPS = 2

current_gain = 0.2
source_gain = 0.5
mixing_side = 0.15
mixing_depth = 0.2
rotation = 0.3
transport = 0.5

LANES = 128
SUBLANES = 8
VMEM = pltpu.VMEM
F32 = jnp.float32
BF16 = jnp.bfloat16


def in_hbm(x):
    return pltpu.with_memory_space_constraint(x, pltpu.HBM)


def lane_chunks(width):
    return range(0, width, LANES)


def spread(columns, r, cols):
    return jnp.broadcast_to(columns[:, r : r + 1], (cols, LANES))


def pack_borders(dims, e_ref, o_ref, odd_col, odd_row, col_refs, row_refs):
    rows, cols, bins, levels, fields = dims

    def pack(spots, to_ref):
        for k in lane_chunks(bins):
            to_ref[:, k : k + LANES] = e_ref[k // LANES, spots, :]
        for q in range(fields):
            to_ref[:, bins + q * levels : bins + (q + 1) * levels] = o_ref[q, spots, :]

    for index, to_ref in enumerate(col_refs):
        near = odd_col if index == 0 else 1 - odd_col
        pack(pl.ds((cols - 1) * (1 - near), rows, stride=cols), to_ref)
    for index, to_ref in enumerate(row_refs):
        near = odd_row if index == 0 else 1 - odd_row
        pack(pl.ds(pl.multiple_of((rows - 1) * cols * (1 - near), cols), cols), to_ref)


def first_kernel(dims, n_col, n_row, parity_ref, e_hbm, o_hbm, e_ref, o_ref, *refs):
    rows, cols, bins, levels, fields = dims
    col_refs = refs[:n_col]
    row_refs = refs[n_col : n_col + n_row]
    sems = refs[-1]
    copies = []
    for k in range(bins // LANES):
        copies.append(
            pltpu.make_async_copy(
                e_hbm.at[:, pl.ds(k * LANES, LANES)], e_ref.at[k], sems.at[k]
            )
        )
    copies.append(pltpu.make_async_copy(o_hbm, o_ref, sems.at[bins // LANES]))
    for copy in copies:
        copy.start()
    for copy in copies:
        copy.wait()
    pack_borders(dims, e_ref, o_ref, parity_ref[0], parity_ref[1], col_refs, row_refs)


def shifted(parts, axis_ids, ahead):
    first, final = axis_ids
    out = []
    if ahead:
        turned = [pltpu.roll(x, SUBLANES - 1, axis=0) for x in parts]
        for i, x in enumerate(turned):
            out.append(jnp.where(final, turned[i + 1] if i + 1 < len(parts) else 0.0, x))
    else:
        turned = [pltpu.roll(x, 1, axis=0) for x in parts]
        for i, x in enumerate(turned):
            out.append(jnp.where(first, turned[i - 1] if i else 0.0, x))
    return out


def sublane_ends():
    ids = lax.broadcasted_iota(jnp.int32, (SUBLANES, LANES), 0)
    return ids == 0, ids == SUBLANES - 1


def advect_all(dims, e_ref, flow_ref, mask_ref, courant_ref, adv_ref):
    rows, cols, bins, levels, fields = dims
    ends = sublane_ends()
    per_row = cols // SUBLANES

    def body(k, _):
        lanes = pl.ds(pl.multiple_of(k * LANES, LANES), LANES)
        speeds = [
            jnp.broadcast_to(courant_ref[way : way + 1, lanes], (SUBLANES, LANES))
            for way in range(2)
        ]

        def load(r):
            if r >= rows:
                return None
            return [
                e_ref[k, r * cols + i * SUBLANES : r * cols + (i + 1) * SUBLANES, :]
                for i in range(per_row)
            ]

        mid = load(0)
        falls = mid
        for r in range(rows):
            following = load(r + 1)
            if following is None:
                falls_next = [-x for x in mid]
            else:
                falls_next = [b - a for a, b in zip(mid, following)]
            west = shifted(mid, ends, False)
            east = shifted(mid, ends, True)
            for i in range(per_row):
                at = slice(r * cols + i * SUBLANES, r * cols + (i + 1) * SUBLANES)
                speed_x = speeds[0] + flow_ref[0, at, :]
                speed_y = speeds[1] + flow_ref[1, at, :]
                flux = speed_x * jnp.where(speed_x > 0, mid[i] - west[i], east[i] - mid[i])
                flux = flux + speed_y * jnp.where(speed_y > 0, falls[i], falls_next[i])
                adv_ref[k, at, :] = mask_ref[at, :] * (mid[i] - flux)
            mid, falls = following, falls_next
        return 0

    lax.fori_loop(0, bins // LANES, body, 0)


def ocean_all(dims, o_ref, mask_ref, part_ref, grad_ref):
    rows, cols, bins, levels, fields = dims
    ends = sublane_ends()
    level_id = lax.broadcasted_iota(jnp.int32, (SUBLANES, levels), 1)
    top = level_id == 0
    bottom = level_id == levels - 1
    per_row = cols // SUBLANES

    def spots(r, i):
        return slice(r * cols + i * SUBLANES, r * cols + (i + 1) * SUBLANES)

    for q in range(fields):
        north = None
        mid = [o_ref[q, spots(0, i), :] for i in range(per_row)]
        for r in range(rows):
            south = None
            if r + 1 < rows:
                south = [o_ref[q, spots(r + 1, i), :] for i in range(per_row)]
            west = shifted(mid, ends, False)
            east = shifted(mid, ends, True)
            for i in range(per_row):
                at = spots(r, i)
                own = mid[i]
                if north is None:
                    across, slope = south[i], south[i]
                elif south is None:
                    across, slope = north[i], -north[i]
                else:
                    across, slope = north[i] + south[i], south[i] - north[i]
                above = jnp.where(top, 0.0, pltpu.roll(own, 1, axis=1))
                below = jnp.where(bottom, 0.0, pltpu.roll(own, levels - 1, axis=1))
                tend = mixing_side * (across + (west[i] + east[i])) + mixing_depth * (above + below)
                tend = tend - (4 * mixing_side + 2 * mixing_depth) * own
                if q == 0:
                    tend = tend + rotation * o_ref[1, at, :]
                elif q == 1:
                    tend = tend - rotation * o_ref[0, at, :]
                else:
                    grad_ref[2 * (q - 2), at, :] = east[i] - west[i]
                    grad_ref[2 * (q - 2) + 1, at, :] = slope
                part_ref[q, at, :] = own + mask_ref[at, :] * tend
            north, mid = mid, south


def window_kernel(dims, first, e_ref, o_ref, *refs):
    rows, cols, bins, levels, fields = dims
    points = rows * cols
    if first:
        mask_t, owner_t, courant_ref, m_hbm, w_hbm = refs[:5]
        adv_ref, part_ref, grad_ref, mask_ref, owner_ref, m_ref, w_ref, flow_ref, sems = refs[5:]
        copies = [
            pltpu.make_async_copy(m_hbm, m_ref, sems.at[0]),
            pltpu.make_async_copy(w_hbm, w_ref, sems.at[1]),
        ]
        for copy in copies:
            copy.start()
        mask = mask_t[...].astype(F32)
        owner = owner_t[...]
        for r in range(rows):
            mask_ref[r * cols : (r + 1) * cols, :] = spread(mask, r, cols)
            owner_ref[r * cols : (r + 1) * cols, :] = spread(owner, r, cols)
    else:
        mask_ref, courant_ref, adv_ref, part_ref, grad_ref, flow_ref = refs
        copies = []
    for way in range(2):
        flow_ref[way] = jnp.broadcast_to(current_gain * o_ref[way, :, 0:1], (points, LANES))
    advect_all(dims, e_ref, flow_ref, mask_ref, courant_ref, adv_ref)
    ocean_all(dims, o_ref, mask_ref, part_ref, grad_ref)
    for copy in copies:
        copy.wait()


def fix_borders(dims, west, east, north, south, o_ref, mask_ref, courant_ref, adv_ref):
    rows, cols, bins, levels, fields = dims
    points = rows * cols

    def column(c, halo, sign):
        sea = mask_ref[pl.ds(c, rows, stride=cols), :]
        speed = o_ref[0, pl.ds(c, rows, stride=cols), :]
        speed = jnp.broadcast_to(current_gain * speed[:, 0:1], (rows, LANES))
        for k in lane_chunks(bins):
            lanes = slice(k, k + LANES)
            flow = jnp.maximum(sign * (courant_ref[0:1, lanes] + speed), 0.0)
            spots = pl.ds(c, rows, stride=cols)
            adv_ref[k // LANES, spots, :] = (
                adv_ref[k // LANES, spots, :] + sea * flow * halo(lanes)
            )

    def row(r, halo, sign):
        sea = mask_ref[r * cols : (r + 1) * cols, :]
        speed = o_ref[1, r * cols : (r + 1) * cols, 0:1]
        speed = jnp.broadcast_to(current_gain * speed, (cols, LANES))
        for k in lane_chunks(bins):
            lanes = slice(k, k + LANES)
            flow = jnp.maximum(sign * (courant_ref[1:2, lanes] + speed), 0.0)
            spots = slice(r * cols, (r + 1) * cols)
            adv_ref[k // LANES, spots, :] = (
                adv_ref[k // LANES, spots, :] + sea * flow * halo(lanes)
            )

    column(0, west, 1.0)
    column(cols - 1, east, -1.0)
    row(0, north, 1.0)
    row(rows - 1, south, -1.0)


def ocean_combine(dims, part_ref, grad_ref, mask_ref, drift_ref, out_ref):
    rows, cols, bins, levels, fields = dims
    sea = mask_ref[...]
    along = sea * drift_ref[0]
    across = sea * drift_ref[1]
    out_ref[0] = part_ref[0] + rotation * across
    out_ref[1] = part_ref[1] - rotation * along
    for q in range(2, fields):
        grad = along * grad_ref[2 * (q - 2)] + across * grad_ref[2 * (q - 2) + 1]
        out_ref[q] = part_ref[q] - (0.5 * transport) * grad


def ocean_borders(dims, west, east, north, south, mask_ref, drift_ref, out_ref):
    rows, cols, bins, levels, fields = dims

    def border(start, count, stride, halo, along, sign):
        spots = pl.ds(start, count, stride=stride)
        sea = mask_ref[spots, :]
        shear = (sign * 0.5 * transport) * drift_ref[along, spots, :]
        for q in range(fields):
            value = halo(slice(bins + q * levels, bins + (q + 1) * levels))
            gain = mixing_side if q < 2 else mixing_side + shear
            out_ref[q, spots, :] = out_ref[q, spots, :] + sea * (gain * value)

    border(0, rows, cols, west, 0, 1.0)
    border(cols - 1, rows, cols, east, 0, -1.0)
    border(0, cols, 1, north, 1, 1.0)
    border((rows - 1) * cols, cols, 1, south, 1, -1.0)


def step_kernel(dims, mats, n_col, n_row, last, parity_ref, adv_old, o_in, part_ref, grad_ref,
                mask_ref, owner_ref, courant_ref, m_ref, w_ref, *refs):
    rows, cols, bins, levels, fields = dims
    chunks = bins // LANES
    got_col = refs[:n_col]
    got_row = refs[n_col : n_col + n_row]
    adv_ref, *rest = refs[n_col + n_row :]
    if last:
        e_hbm, o_hbm, low_ref, drift_ref, e_ref, o_ref, sems = rest
    else:
        e_ref, o_ref = rest[:2]
        col_refs = rest[2 : 2 + n_col]
        row_refs = rest[2 + n_col : 2 + n_col + n_row]
        low_ref, drift_ref = rest[2 + n_col + n_row :]
    odd_col = parity_ref[0] == 1
    odd_row = parity_ref[1] == 1

    def halo(got, odd, before):
        first = got[0]
        second = got[1] if len(got) > 1 else None

        def read(lanes):
            def take(ref):
                return 0.0 if ref is None else ref[:, lanes]

            if before:
                return jnp.where(odd, take(first), take(second))
            return jnp.where(odd, take(second), take(first))

        return read

    west = halo(got_col, odd_col, True)
    east = halo(got_col, odd_col, False)
    north = halo(got_row, odd_row, True)
    south = halo(got_row, odd_row, False)

    fix_borders(dims, west, east, north, south, o_in, mask_ref, courant_ref, adv_ref)
    owner = owner_ref[...]
    low = jnp.concatenate(
        [
            jnp.where(owner == m, adv_ref[k], 0.0).astype(BF16)
            for m in range(mats)
            for k in range(chunks)
        ],
        axis=1,
    )
    weights = jnp.concatenate([m_ref[m] for m in range(mats)], axis=1)
    source = lax.dot_general(
        low, weights, (((1,), (1,)), ((), ())), preferred_element_type=F32
    )
    sea = mask_ref[...]
    for k in range(chunks):
        lanes = slice(k * LANES, (k + 1) * LANES)
        energy = sea * (adv_ref[k] + source_gain * source[:, lanes])
        if last:
            e_ref[:, lanes] = energy
        else:
            e_ref[k] = energy
        low_ref[:, lanes] = energy.astype(BF16)
    if last:
        e_copy = pltpu.make_async_copy(e_ref, e_hbm, sems.at[0])
        e_copy.start()
    drift = jnp.dot(low_ref[...], w_ref[...], preferred_element_type=F32)
    for k in range(2):
        drift_ref[k] = drift[:, k * levels : (k + 1) * levels]
    ocean_combine(dims, part_ref, grad_ref, mask_ref, drift_ref, o_ref)
    ocean_borders(dims, west, east, north, south, mask_ref, drift_ref, o_ref)
    if last:
        o_copy = pltpu.make_async_copy(o_ref, o_hbm, sems.at[1])
        o_copy.start()
        e_copy.wait()
        o_copy.wait()
    else:
        pack_borders(dims, e_ref, o_ref, parity_ref[0], parity_ref[1], col_refs, row_refs)


def swap_pairs(values, axis):
    count = lax.axis_size(axis)
    got = []
    for index, value in enumerate(values):
        pairs = []
        for i in range(index, count - 1, 2):
            pairs += [(i, i + 1), (i + 1, i)]
        got.append(lax.ppermute(value, axis, pairs))
    return got


def local(spectrum, matrices, ownership, land_mask, courant, stokes_weight, ocean):
    bins, rows, cols = spectrum.shape
    fields, _, _, levels = ocean.shape
    mats = matrices.shape[2]
    points = rows * cols
    dims = (rows, cols, bins, levels, fields)
    n_col = 2 if lax.axis_size("grp") > 2 else 1
    n_row = 2 if lax.axis_size("tile") > 2 else 1
    e0 = jnp.transpose(spectrum, (1, 2, 0)).reshape(points, bins)
    o0 = ocean.reshape(fields, points, levels)
    m0 = matrices.reshape(mats, bins, bins)
    mask_t = land_mask.T
    owner_t = ownership.T
    parity = jnp.stack([lax.axis_index("grp") % 2, lax.axis_index("tile") % 2]).astype(jnp.int32)

    vmem = pl.BlockSpec(memory_space=VMEM)
    smem = pl.BlockSpec(memory_space=pltpu.SMEM)
    hbm = pl.BlockSpec(memory_space=pltpu.HBM)
    chunks = bins // LANES
    e_shape = VMEM((chunks, points, LANES), F32)
    o_shape = VMEM((fields, points, levels), F32)
    part_shapes = [e_shape, o_shape, VMEM((2 * (fields - 2), points, levels), F32)]
    wide = bins + fields * levels
    borders = [VMEM((rows, wide), F32)] * n_col + [VMEM((cols, wide), F32)] * n_row
    flow = VMEM((2, points, LANES), F32)
    n_all = n_col + n_row

    def params(mib):
        return pltpu.CompilerParams(vmem_limit_bytes=mib * 2**20)

    def exchange(sent):
        return swap_pairs(sent[:n_col], "grp") + swap_pairs(sent[n_col:], "tile")

    e, o, *sent = pl.pallas_call(
        functools.partial(first_kernel, dims, n_col, n_row),
        out_shape=[e_shape, o_shape] + borders,
        in_specs=[smem, hbm, hbm],
        out_specs=[vmem] * (2 + n_all),
        scratch_shapes=[pltpu.SemaphoreType.DMA((chunks + 1,))],
        compiler_params=params(8),
        name="first",
    )(parity, in_hbm(e0), in_hbm(o0))
    for step in range(STEPS):
        got = exchange(sent)
        if step == 0:
            adv, part, grad, mask, owner, m, w = pl.pallas_call(
                functools.partial(window_kernel, dims, True),
                out_shape=part_shapes
                + [
                    VMEM((points, LANES), F32),
                    VMEM((points, LANES), jnp.int32),
                    VMEM((mats, bins, bins), BF16),
                    VMEM(stokes_weight.shape, BF16),
                ],
                in_specs=[vmem] * 5 + [hbm] * 2,
                out_specs=[vmem] * 7,
                scratch_shapes=[flow, pltpu.SemaphoreType.DMA((2,))],
                compiler_params=params(16),
                name="window_first",
            )(e, o, mask_t, owner_t, courant, in_hbm(m0), in_hbm(stokes_weight))
        else:
            adv, part, grad = pl.pallas_call(
                functools.partial(window_kernel, dims, False),
                out_shape=part_shapes,
                in_specs=[vmem] * 4,
                out_specs=[vmem] * 3,
                scratch_shapes=[flow],
                compiler_params=params(16),
                name="window",
            )(e, o, mask, courant)
        last = step == STEPS - 1
        scratch = [VMEM((points, bins), BF16), VMEM((2, points, levels), F32)]
        if last:
            out_shape = [
                jax.ShapeDtypeStruct((points, bins), F32),
                jax.ShapeDtypeStruct((fields, points, levels), F32),
            ]
            out_specs = [hbm, hbm]
            scratch += [
                VMEM((points, bins), F32),
                VMEM((fields, points, levels), F32),
                pltpu.SemaphoreType.DMA((2,)),
            ]
        else:
            out_shape = [e_shape, o_shape] + borders
            out_specs = [vmem] * (2 + n_all)
        out = pl.pallas_call(
            functools.partial(step_kernel, dims, mats, n_col, n_row, last),
            out_shape=[e_shape] + out_shape,
            in_specs=[smem] + [vmem] * (9 + n_all),
            out_specs=[vmem] + out_specs,
            scratch_shapes=scratch,
            input_output_aliases={1: 0},
            compiler_params=params(32),
            name="step_last" if last else "step",
        )(parity, adv, o, part, grad, mask, owner, courant, m, w, *got)
        if last:
            _, energy, fields_out = out
        else:
            _, e, o, *sent = out
    energy = jnp.transpose(energy.reshape(rows, cols, bins), (2, 0, 1))
    return energy, fields_out.reshape(ocean.shape)


def solution(mesh):
    in_specs = (
        P(None, "tile", "grp"),
        P("tile", "grp", None, None, None),
        P("tile", "grp"),
        P("tile", "grp"),
        P(),
        P(),
        P(None, "tile", "grp", None),
    )
    out_specs = (P(None, "tile", "grp"), P(None, "tile", "grp", None))
    return jax.shard_map(local, mesh=mesh, in_specs=in_specs, out_specs=out_specs, check_vma=False)
```

```python
import functools

import jax
import jax.numpy as jnp
from jax import lax
from jax.experimental import pallas as pl
from jax.experimental.pallas import tpu as pltpu
from jax.sharding import PartitionSpec as P

STEPS = 2

current_gain = 0.2
source_gain = 0.5
mixing_side = 0.15
mixing_depth = 0.2
rotation = 0.3
transport = 0.5

LANES = 128
SUBLANES = 8
VMEM = pltpu.VMEM
F32 = jnp.float32
BF16 = jnp.bfloat16


def in_hbm(x):
    return pltpu.with_memory_space_constraint(x, pltpu.HBM)


def lane_chunks(width):
    return range(0, width, LANES)


def spread(columns, r, cols):
    return jnp.broadcast_to(columns[:, r : r + 1], (cols, LANES))


def low_side(parity, index):
    return parity if index == 0 else 1 - parity


def column_place(dims, parity, index):
    rows, cols, bins, levels, fields = dims
    high = 1 - low_side(parity, index)
    tile = high * (cols // SUBLANES - 1)
    return tile, pl.ds(high * (SUBLANES - 1), rows, stride=SUBLANES)


def row_place(dims, parity, index):
    high = 1 - low_side(parity, index)
    return pl.ds(pl.multiple_of(high * (dims[0] - 1) * SUBLANES, SUBLANES), SUBLANES)


def side_sign(parity, index):
    return jnp.where(low_side(parity, index) == 1, 1.0, -1.0).astype(F32)


def first_kernel(dims, n_col, n_row, parity_ref, e_hbm, o_hbm, *refs):
    rows, cols, bins, levels, fields = dims
    col_refs = refs[:n_col]
    row_refs = refs[n_col : n_col + n_row]
    sems = refs[-1]

    def pieces(to_ref, e_from, o_from, slot):
        copies = [pltpu.make_async_copy(e_from, to_ref.at[..., 0:bins], sems.at[slot, 0])]
        for q in range(fields):
            lanes = pl.ds(bins + q * levels, levels)
            copies.append(
                pltpu.make_async_copy(o_from(q), to_ref.at[..., lanes], sems.at[slot, 1 + q])
            )
        return copies

    def column(index, high):
        tile = high * (cols // SUBLANES - 1)
        place = high * (SUBLANES - 1)
        return pieces(
            col_refs[index],
            e_hbm.at[:, tile, place, :],
            lambda q: o_hbm.at[q, :, tile, place, :],
            index,
        )

    def row(index):
        r = (1 - low_side(parity_ref[1], index)) * (rows - 1)
        return pieces(row_refs[index], e_hbm.at[r], lambda q: o_hbm.at[q, r], n_col + index)

    for odd in range(2):

        @pl.when(parity_ref[0] == odd)
        def _(odd=odd):
            for index in reversed(range(n_col)):
                for copy in column(index, 1 - low_side(odd, index)):
                    copy.start()

    for index in range(n_row):
        for copy in row(index):
            copy.start()
    for index in range(n_col):
        for copy in column(index, 0):
            copy.wait()
    for index in range(n_row):
        for copy in row(index):
            copy.wait()


def shifted(parts, axis_ids, ahead):
    first, final = axis_ids
    out = []
    if ahead:
        turned = [pltpu.roll(x, SUBLANES - 1, axis=0) for x in parts]
        for i, x in enumerate(turned):
            out.append(jnp.where(final, turned[i + 1] if i + 1 < len(parts) else 0.0, x))
    else:
        turned = [pltpu.roll(x, 1, axis=0) for x in parts]
        for i, x in enumerate(turned):
            out.append(jnp.where(first, turned[i - 1] if i else 0.0, x))
    return out


def sublane_ends():
    ids = lax.broadcasted_iota(jnp.int32, (SUBLANES, LANES), 0)
    return ids == 0, ids == SUBLANES - 1


def span(r):
    return slice(r * SUBLANES, (r + 1) * SUBLANES)


def tile_at(ref, lead, i, r):
    if ref.ndim == 5:
        return ref[lead, i, r]
    return ref[lead, i, span(r), :]


def advect_all(dims, e_ref, arrived, flow_ref, mask_ref, courant_ref, adv_ref):
    rows, cols, bins, levels, fields = dims
    ends = sublane_ends()
    tiles = cols // SUBLANES

    def body(k, _):
        arrived(k)
        lanes = pl.ds(pl.multiple_of(k * LANES, LANES), LANES)
        speeds = [
            jnp.broadcast_to(courant_ref[way : way + 1, lanes], (SUBLANES, LANES))
            for way in range(2)
        ]

        def load(r):
            if r >= rows:
                return None
            return [tile_at(e_ref, k, i, r) for i in range(tiles)]

        mid = load(0)
        falls = mid
        for r in range(rows):
            following = load(r + 1)
            if following is None:
                falls_next = [-x for x in mid]
            else:
                falls_next = [b - a for a, b in zip(mid, following)]
            west = shifted(mid, ends, False)
            east = shifted(mid, ends, True)
            for i in range(tiles):
                speed_x = speeds[0] + flow_ref[0, i, span(r), :]
                speed_y = speeds[1] + flow_ref[1, i, span(r), :]
                flux = speed_x * jnp.where(speed_x > 0, mid[i] - west[i], east[i] - mid[i])
                flux = flux + speed_y * jnp.where(speed_y > 0, falls[i], falls_next[i])
                adv_ref[k, i, span(r), :] = mask_ref[i, span(r), :] * (mid[i] - flux)
            mid, falls = following, falls_next
        return 0

    lax.fori_loop(0, bins // LANES, body, 0)


def ocean_all(dims, o_ref, mask_ref, part_ref, grad_ref):
    rows, cols, bins, levels, fields = dims
    ends = sublane_ends()
    level_id = lax.broadcasted_iota(jnp.int32, (SUBLANES, levels), 1)
    top = level_id == 0
    bottom = level_id == levels - 1
    tiles = cols // SUBLANES

    for q in range(fields):
        north = None
        mid = [tile_at(o_ref, q, i, 0) for i in range(tiles)]
        for r in range(rows):
            south = None
            if r + 1 < rows:
                south = [tile_at(o_ref, q, i, r + 1) for i in range(tiles)]
            west = shifted(mid, ends, False)
            east = shifted(mid, ends, True)
            for i in range(tiles):
                own = mid[i]
                if north is None:
                    across, slope = south[i], south[i]
                elif south is None:
                    across, slope = north[i], -north[i]
                else:
                    across, slope = north[i] + south[i], south[i] - north[i]
                above = jnp.where(top, 0.0, pltpu.roll(own, 1, axis=1))
                below = jnp.where(bottom, 0.0, pltpu.roll(own, levels - 1, axis=1))
                tend = mixing_side * (across + (west[i] + east[i])) + mixing_depth * (above + below)
                tend = tend - (4 * mixing_side + 2 * mixing_depth) * own
                if q == 0:
                    tend = tend + rotation * tile_at(o_ref, 1, i, r)
                elif q == 1:
                    tend = tend - rotation * tile_at(o_ref, 0, i, r)
                else:
                    grad_ref[2 * (q - 2), i, span(r), :] = east[i] - west[i]
                    grad_ref[2 * (q - 2) + 1, i, span(r), :] = slope
                part_ref[q, i, span(r), :] = own + mask_ref[i, span(r), :] * tend
            north, mid = mid, south


def window_kernel(dims, first, e_in, o_in, *refs):
    rows, cols, bins, levels, fields = dims
    tiles = cols // SUBLANES
    if first:
        mask_t, owner_t, courant_ref, m_hbm, w_hbm = refs[:5]
        adv_ref, part_ref, grad_ref, flow_ref, mask_ref, owner_ref, m_ref, w_ref = refs[5:13]
        e_ref, o_ref, e_sems, o_sems, m_sems = refs[13:]

        def e_copies(k):
            lanes = pl.ds(pl.multiple_of(k * LANES, LANES), LANES)
            return [
                pltpu.make_async_copy(
                    e_in.at[:, i, :, lanes], e_ref.at[k, i], e_sems.at[k, i]
                )
                for i in range(tiles)
            ]

        o_copies = [
            pltpu.make_async_copy(o_in.at[q, :, i], o_ref.at[q, i], o_sems.at[q, i])
            for q in range(fields)
            for i in range(tiles)
        ]
        m_copies = [
            pltpu.make_async_copy(m_hbm, m_ref, m_sems.at[0]),
            pltpu.make_async_copy(w_hbm, w_ref, m_sems.at[1]),
        ]
        for copy in o_copies:
            copy.start()
        for k in range(bins // LANES):
            for copy in e_copies(k):
                copy.start()
        for copy in m_copies:
            copy.start()
        mask = mask_t[...].astype(F32)
        owner = owner_t[...]
        for i in range(tiles):
            for r in range(rows):
                for to_ref, values in ((mask_ref, mask), (owner_ref, owner)):
                    to_ref[i, span(r), :] = jnp.broadcast_to(
                        values[span(i), r : r + 1], (SUBLANES, LANES)
                    )
        for copy in o_copies:
            copy.wait()
    else:
        mask_ref, courant_ref, adv_ref, part_ref, grad_ref, flow_ref = refs
        e_ref, o_ref = e_in, o_in
        m_copies = []

    def arrived(k):
        if first:
            for copy in e_copies(k):
                copy.wait()

    for way in range(2):
        for i in range(tiles):
            for r in range(rows):
                current = tile_at(o_ref, way, i, r)
                flow_ref[way, i, span(r), :] = jnp.broadcast_to(
                    current_gain * current[:, 0:1], (SUBLANES, LANES)
                )
    ocean_all(dims, o_ref, mask_ref, part_ref, grad_ref)
    advect_all(dims, e_ref, arrived, flow_ref, mask_ref, courant_ref, adv_ref)
    for copy in m_copies:
        copy.wait()


def fix_column(dims, parity, index, halo_ref, flow_ref, mask_ref, courant_ref, adv_ref):
    tile, spots = column_place(dims, parity, index)
    sign = side_sign(parity, index)
    sea = mask_ref[tile, spots, :]
    speed = flow_ref[0, tile, spots, :]
    for k in range(dims[2] // LANES):
        lanes = slice(k * LANES, (k + 1) * LANES)
        inward = jnp.maximum(sign * (courant_ref[0:1, lanes] + speed), 0.0)
        adv_ref[k, tile, spots, :] = (
            adv_ref[k, tile, spots, :] + sea * inward * halo_ref[:, lanes]
        )


def fix_row(dims, parity, index, halo_ref, flow_ref, mask_ref, courant_ref, adv_ref):
    spots = row_place(dims, parity, index)
    sign = side_sign(parity, index)
    for i in range(dims[1] // SUBLANES):
        sea = mask_ref[i, spots, :]
        speed = flow_ref[1, i, spots, :]
        for k in range(dims[2] // LANES):
            lanes = slice(k * LANES, (k + 1) * LANES)
            inward = jnp.maximum(sign * (courant_ref[1:2, lanes] + speed), 0.0)
            adv_ref[k, i, spots, :] = (
                adv_ref[k, i, spots, :] + sea * inward * halo_ref[i, :, lanes]
            )


def ocean_border(dims, sign, along, tile, spots, halo, mask_ref, drift_ref, out_ref):
    rows, cols, bins, levels, fields = dims
    sea = mask_ref[tile, spots, :]
    shear = (sign * (0.5 * transport)) * drift_ref[along, spots, :]
    for q in range(fields):
        value = halo(slice(bins + q * levels, bins + (q + 1) * levels))
        gain = mixing_side if q < 2 else mixing_side + shear
        out_ref[q, spots, :] = out_ref[q, spots, :] + sea * (gain * value)


def source_of(dims, mats, tile, adv_ref, owner_ref, m_ref):
    chunks = dims[2] // LANES
    owner = owner_ref[tile]
    low = jnp.concatenate(
        [
            jnp.where(owner == m, adv_ref[k, tile], 0.0).astype(BF16)
            for m in range(mats)
            for k in range(chunks)
        ],
        axis=1,
    )
    weights = jnp.concatenate([m_ref[m] for m in range(mats)], axis=1)
    return lax.dot_general(low, weights, (((1,), (1,)), ((), ())), preferred_element_type=F32)


def ocean_tile(dims, tile, col_border, row_borders, parity, part_ref, grad_ref, mask_ref,
               w_ref, low_ref, drift_ref, out_ref):
    rows, cols, bins, levels, fields = dims
    drift = jnp.dot(low_ref[...], w_ref[...], preferred_element_type=F32)
    for k in range(2):
        drift_ref[k] = drift[:, k * levels : (k + 1) * levels]
    sea = mask_ref[tile]
    along = sea * drift[:, 0:levels]
    across = sea * drift[:, levels : 2 * levels]
    out_ref[0] = part_ref[0, tile] + rotation * across
    out_ref[1] = part_ref[1, tile] - rotation * along
    for q in range(2, fields):
        grad = along * grad_ref[2 * (q - 2), tile] + across * grad_ref[2 * (q - 2) + 1, tile]
        out_ref[q] = part_ref[q, tile] - (0.5 * transport) * grad
    if col_border is not None:
        index, halo_ref = col_border
        _, spots = column_place(dims, parity[0], index)
        ocean_border(
            dims, side_sign(parity[0], index), 0, tile, spots, lambda lanes: halo_ref[:, lanes],
            mask_ref, drift_ref, out_ref,
        )
    for index, halo_ref in enumerate(row_borders):
        ocean_border(
            dims, side_sign(parity[1], index), 1, tile, row_place(dims, parity[1], index),
            lambda lanes: halo_ref[tile, :, lanes], mask_ref, drift_ref, out_ref,
        )


def step_kernel(dims, mats, late, last, n_col, n_row, *refs):
    rows, cols, bins, levels, fields = dims
    tiles = cols // SUBLANES
    parity_ref, courant_ref, adv_in, part_ref, grad_ref, flow_ref = refs[:6]
    mask_ref, owner_ref, m_ref, w_ref = refs[6:10]
    refs = refs[10:]
    got_col, got_row, refs = refs[0], refs[1 : 1 + n_row], refs[1 + n_row :]
    if late:
        refs = refs[2:]
    adv_ref, e_out, o_out, *refs = refs
    if late and not last:
        col_refs, row_refs, refs = refs[:n_col], refs[n_col : n_col + n_row], refs[n_col + n_row :]
    if last:
        low_ref, drift_ref, e_tile, o_tile, sems = refs
    else:
        low_ref, drift_ref = refs
    parity = parity_ref[0], parity_ref[1]
    index = 1 if late else 0
    fixed = (flow_ref, mask_ref, courant_ref, adv_ref)
    if not late:
        for row_index in range(n_row):
            fix_row(dims, parity[1], row_index, got_row[row_index], *fixed)
    fix_column(dims, parity[0], index, got_col, *fixed)
    late_tile = (1 - low_side(parity[0], 1)) * (tiles - 1)
    if late:
        todo = [late_tile]
    else:
        walk = parity[0]
        todo = [walk * i + (1 - walk) * (tiles - 1 - i) for i in range(tiles - 1)]
    for number, tile in enumerate(todo):
        source = source_of(dims, mats, tile, adv_ref, owner_ref, m_ref)
        sea = mask_ref[tile]
        for k in range(bins // LANES):
            lanes = slice(k * LANES, (k + 1) * LANES)
            energy = sea * (adv_ref[k, tile] + source_gain * source[:, lanes])
            if last:
                e_tile[:, :, lanes] = energy.reshape(rows, SUBLANES, LANES)
            else:
                e_out[k, tile] = energy
            low_ref[:, lanes] = energy.astype(BF16)
        if last:
            e_copy = pltpu.make_async_copy(e_tile, e_out.at[:, tile], sems.at[0])
            e_copy.start()
        out_ref = o_tile if last else o_out.at[:, tile]
        ocean_tile(
            dims, tile, (index, got_col) if number == 0 else None, got_row, parity, part_ref, grad_ref, mask_ref,
            w_ref, low_ref, drift_ref, out_ref,
        )
        if last:
            o_copies = [
                pltpu.make_async_copy(
                    o_tile.at[q].reshape(rows, SUBLANES, levels), o_out.at[q, :, tile], sems.at[1 + q]
                )
                for q in range(fields)
            ]
            for copy in o_copies:
                copy.start()
            e_copy.wait()
            for copy in o_copies:
                copy.wait()
    if late and not last:

        def pack(to_ref, take):
            for k in lane_chunks(bins):
                to_ref[..., k : k + LANES] = take(e_out.at[k // LANES])
            for q in range(fields):
                to_ref[..., bins + q * levels : bins + (q + 1) * levels] = take(o_out.at[q])

        for i, to_ref in enumerate(col_refs):
            tile, spots = column_place(dims, parity[0], i)
            pack(to_ref, lambda ref: ref[tile, spots, :])
        for i, to_ref in enumerate(row_refs):
            spots = row_place(dims, parity[1], i)
            pack(to_ref, lambda ref: ref[:, spots, :])


def swap_pairs(values, axis):
    count = lax.axis_size(axis)
    got = []
    for index, value in enumerate(values):
        pairs = []
        for i in range(index, count - 1, 2):
            pairs += [(i, i + 1), (i + 1, i)]
        got.append(lax.ppermute(value, axis, pairs))
    return got


def local(spectrum, matrices, ownership, land_mask, courant, stokes_weight, ocean):
    bins, rows, cols = spectrum.shape
    fields, _, _, levels = ocean.shape
    mats = matrices.shape[2]
    tiles = cols // SUBLANES
    chunks = bins // LANES
    dims = (rows, cols, bins, levels, fields)
    n_col = 2
    n_row = 2 if lax.axis_size("tile") > 2 else 1
    e0 = jnp.transpose(spectrum, (1, 2, 0)).reshape(rows, tiles, SUBLANES, bins)
    o0 = ocean.reshape(fields, rows, tiles, SUBLANES, levels)
    m0 = matrices.reshape(mats, bins, bins)
    mask_t = land_mask.T
    owner_t = ownership.T
    parity = jnp.stack([lax.axis_index("grp") % 2, lax.axis_index("tile") % 2]).astype(jnp.int32)

    vmem = pl.BlockSpec(memory_space=VMEM)
    smem = pl.BlockSpec(memory_space=pltpu.SMEM)
    hbm = pl.BlockSpec(memory_space=pltpu.HBM)

    def points(lead, width=LANES, dtype=F32):
        return VMEM((*lead, tiles, rows * SUBLANES, width), dtype)

    adv_shape = points((chunks,))
    o_shape = points((fields,), levels)
    window_shapes = [adv_shape, o_shape, points((2 * (fields - 2),), levels), points((2,))]
    wide = bins + fields * levels
    borders = [VMEM((rows, wide), F32)] * n_col + [VMEM((tiles, SUBLANES, wide), F32)] * n_row
    dma = pltpu.SemaphoreType.DMA

    def params(mib):
        return pltpu.CompilerParams(vmem_limit_bytes=mib * 2**20)

    def exchange(sent):
        return swap_pairs(sent[:n_col], "grp") + swap_pairs(sent[n_col:], "tile")

    sent = pl.pallas_call(
        functools.partial(first_kernel, dims, n_col, n_row),
        out_shape=borders,
        in_specs=[smem, hbm, hbm],
        out_specs=[vmem] * len(borders),
        scratch_shapes=[dma((n_col + n_row, 1 + fields))],
        compiler_params=params(8),
        name="first",
    )(parity, in_hbm(e0), in_hbm(o0))
    e = o = None
    for step in range(STEPS):
        got = exchange(sent)
        if step == 0:
            adv, part, grad, flow, mask, owner, m, w = pl.pallas_call(
                functools.partial(window_kernel, dims, True),
                out_shape=window_shapes
                + [
                    points(()),
                    points((), LANES, jnp.int32),
                    VMEM((mats, bins, bins), BF16),
                    VMEM(stokes_weight.shape, BF16),
                ],
                in_specs=[hbm] * 2 + [vmem] * 3 + [hbm] * 2,
                out_specs=[vmem] * 8,
                scratch_shapes=[
                    VMEM((chunks, tiles, rows, SUBLANES, LANES), F32),
                    VMEM((fields, tiles, rows, SUBLANES, levels), F32),
                    dma((chunks, tiles)),
                    dma((fields, tiles)),
                    dma((2,)),
                ],
                compiler_params=params(16),
                name="window_first",
            )(
                in_hbm(e0), in_hbm(o0), mask_t, owner_t, courant, in_hbm(m0),
                in_hbm(stokes_weight),
            )
        else:
            adv, part, grad, flow = pl.pallas_call(
                functools.partial(window_kernel, dims, False),
                out_shape=window_shapes,
                in_specs=[vmem] * 4,
                out_specs=[vmem] * 4,
                compiler_params=params(16),
                name="window",
            )(e, o, mask, courant)
        last = step == STEPS - 1
        scratch = [VMEM((rows * SUBLANES, bins), BF16), VMEM((2, rows * SUBLANES, levels), F32)]
        if last:
            out_shape = [
                adv_shape,
                pltpu.HBM(e0.shape, F32),
                pltpu.HBM(o0.shape, F32),
            ]
            out_specs = [vmem, hbm, hbm]
            scratch += [
                VMEM((rows, SUBLANES, bins), F32),
                VMEM((fields, rows * SUBLANES, levels), F32),
                dma((1 + fields,)),
            ]
        else:
            out_shape = [adv_shape, adv_shape, o_shape]
            out_specs = [vmem] * 3
        common = (mask, owner, m, w)
        adv, e, o = pl.pallas_call(
            functools.partial(step_kernel, dims, mats, False, last, n_col, n_row),
            out_shape=out_shape,
            in_specs=[smem] + [vmem] * (10 + n_row),
            out_specs=out_specs,
            scratch_shapes=scratch,
            input_output_aliases={2: 0},
            compiler_params=params(24),
            name="early_last" if last else "early",
        )(parity, courant, adv, part, grad, flow, *common, got[0], *got[n_col:])
        extra = [] if last else borders
        e_at = 11 + n_row
        _, e, o, *sent = pl.pallas_call(
            functools.partial(step_kernel, dims, mats, True, last, n_col, n_row),
            out_shape=out_shape + extra,
            in_specs=[smem] + [vmem] * (10 + n_row) + out_specs[1:],
            out_specs=out_specs + [vmem] * len(extra),
            scratch_shapes=scratch,
            input_output_aliases={2: 0, e_at: 1, e_at + 1: 2},
            compiler_params=params(24),
            name="late_last" if last else "late",
        )(parity, courant, adv, part, grad, flow, *common, got[1], *got[n_col:], e, o)
    energy = jnp.transpose(e.reshape(rows, cols, bins), (2, 0, 1))
    return energy, o.reshape(ocean.shape)


def solution(mesh):
    in_specs = (
        P(None, "tile", "grp"),
        P("tile", "grp", None, None, None),
        P("tile", "grp"),
        P("tile", "grp"),
        P(),
        P(),
        P(None, "tile", "grp", None),
    )
    out_specs = (P(None, "tile", "grp"), P(None, "tile", "grp", None))
    return jax.shard_map(local, mesh=mesh, in_specs=in_specs, out_specs=out_specs, check_vma=False)
```

```python
import functools

import jax
import jax.numpy as jnp
from jax import lax
from jax.experimental import pallas as pl
from jax.experimental.pallas import tpu as pltpu
from jax.sharding import PartitionSpec as P


STEPS = 2

current_gain = 0.2
source_gain = 0.5
mixing_side = 0.15
mixing_depth = 0.2
rotation = 0.3
transport = 0.5

LANES = 128
SUBLANES = 8
VMEM = pltpu.VMEM
F32 = jnp.float32
BF16 = jnp.bfloat16


def in_hbm(x):
    return pltpu.with_memory_space_constraint(x, pltpu.HBM)


def lane_chunks(width):
    return range(0, width, LANES)


def low_side(parity, index):
    return parity if index == 0 else 1 - parity


def column_place(dims, parity, index):
    rows, cols, _, _, _ = dims
    high = 1 - low_side(parity, index)
    tile = high * (cols // SUBLANES - 1)
    return tile, pl.ds(high * (SUBLANES - 1), rows, stride=SUBLANES)


def row_place(dims, parity, index):
    high = 1 - low_side(parity, index)
    return pl.ds(pl.multiple_of(high * (dims[0] - 1) * SUBLANES, SUBLANES), SUBLANES)


def side_sign(parity, index):
    return jnp.where(low_side(parity, index) == 1, 1.0, -1.0).astype(F32)


def first_kernel(dims, n_col, n_row, parity_ref, e_hbm, o_hbm, *refs):
    rows, cols, bins, levels, fields = dims
    col_refs = refs[:n_col]
    row_refs = refs[n_col : n_col + n_row]
    sems = refs[-1]

    def pieces(to_ref, e_from, o_from, slot):
        copies = [pltpu.make_async_copy(e_from, to_ref.at[..., 0:bins], sems.at[slot, 0])]
        for q in range(fields):
            lanes = pl.ds(bins + q * levels, levels)
            copies.append(
                pltpu.make_async_copy(o_from(q), to_ref.at[..., lanes], sems.at[slot, 1 + q])
            )
        return copies

    def column(index, high):
        tile = high * (cols // SUBLANES - 1)
        place = high * (SUBLANES - 1)
        return pieces(
            col_refs[index],
            e_hbm.at[:, tile, place, :],
            lambda q: o_hbm.at[q, :, tile, place, :],
            index,
        )

    def row(index):
        r = (1 - low_side(parity_ref[1], index)) * (rows - 1)
        return pieces(row_refs[index], e_hbm.at[r], lambda q: o_hbm.at[q, r], n_col + index)

    for odd in range(2):

        @pl.when(parity_ref[0] == odd)
        def _(odd=odd):
            for index in reversed(range(n_col)):
                for copy in column(index, 1 - low_side(odd, index)):
                    copy.start()

    for index in range(n_row):
        for copy in row(index):
            copy.start()
    for index in range(n_col):
        for copy in column(index, 0):
            copy.wait()
    for index in range(n_row):
        for copy in row(index):
            copy.wait()


def shifted(parts, axis_ids, ahead):
    first, final = axis_ids
    out = []
    if ahead:
        turned = [pltpu.roll(x, SUBLANES - 1, axis=0) for x in parts]
        for i, x in enumerate(turned):
            out.append(jnp.where(final, turned[i + 1] if i + 1 < len(parts) else 0.0, x))
    else:
        turned = [pltpu.roll(x, 1, axis=0) for x in parts]
        for i, x in enumerate(turned):
            out.append(jnp.where(first, turned[i - 1] if i else 0.0, x))
    return out


def sublane_ends():
    ids = lax.broadcasted_iota(jnp.int32, (SUBLANES, LANES), 0)
    return ids == 0, ids == SUBLANES - 1


def span(r):
    return slice(r * SUBLANES, (r + 1) * SUBLANES)


def advect_all(dims, energy_at, arrived, flow_ref, mask_ref, courant_ref, adv_ref):
    rows, cols, bins, _, _ = dims
    ends = sublane_ends()
    tiles = cols // SUBLANES

    def body(k, _):
        arrived(k)
        lanes = pl.ds(pl.multiple_of(k * LANES, LANES), LANES)
        speeds = [
            jnp.broadcast_to(courant_ref[way : way + 1, lanes], (SUBLANES, LANES))
            for way in range(2)
        ]

        def load(r):
            if r >= rows:
                return None
            return [energy_at(k, i, r) for i in range(tiles)]

        mid = load(0)
        falls = mid
        for r in range(rows):
            following = load(r + 1)
            if following is None:
                falls_next = [-x for x in mid]
            else:
                falls_next = [b - a for a, b in zip(mid, following)]
            west = shifted(mid, ends, False)
            east = shifted(mid, ends, True)
            for i in range(tiles):
                speed_x = speeds[0] + flow_ref[0, i, span(r), :]
                speed_y = speeds[1] + flow_ref[1, i, span(r), :]
                flux = speed_x * jnp.where(speed_x > 0, mid[i] - west[i], east[i] - mid[i])
                flux = flux + speed_y * jnp.where(speed_y > 0, falls[i], falls_next[i])
                adv_ref[k, i, span(r), :] = mask_ref[i, span(r), :] * (mid[i] - flux)
            mid, falls = following, falls_next
        return 0

    lax.fori_loop(0, bins // LANES, body, 0)


def ocean_all(dims, ocean_at, mask_ref, part_ref, grad_ref):
    rows, cols, _, levels, fields = dims
    ends = sublane_ends()
    level_id = lax.broadcasted_iota(jnp.int32, (SUBLANES, levels), 1)
    top = level_id == 0
    bottom = level_id == levels - 1
    tiles = cols // SUBLANES

    for q in range(fields):
        north = None
        mid = [ocean_at(q, i, 0) for i in range(tiles)]
        for r in range(rows):
            south = None
            if r + 1 < rows:
                south = [ocean_at(q, i, r + 1) for i in range(tiles)]
            west = shifted(mid, ends, False)
            east = shifted(mid, ends, True)
            for i in range(tiles):
                own = mid[i]
                if north is None:
                    across, slope = south[i], south[i]
                elif south is None:
                    across, slope = north[i], -north[i]
                else:
                    across, slope = north[i] + south[i], south[i] - north[i]
                above = jnp.where(top, 0.0, pltpu.roll(own, 1, axis=1))
                below = jnp.where(bottom, 0.0, pltpu.roll(own, levels - 1, axis=1))
                tend = mixing_side * (across + (west[i] + east[i])) + mixing_depth * (above + below)
                tend = tend - (4 * mixing_side + 2 * mixing_depth) * own
                if q == 0:
                    tend = tend + rotation * ocean_at(1, i, r)
                elif q == 1:
                    tend = tend - rotation * ocean_at(0, i, r)
                else:
                    grad_ref[2 * (q - 2), i, span(r), :] = east[i] - west[i]
                    grad_ref[2 * (q - 2) + 1, i, span(r), :] = slope
                part_ref[q, i, span(r), :] = own + mask_ref[i, span(r), :] * tend
            north, mid = mid, south


def window_kernel(dims, first, e_ref, o_ref, *refs):
    rows, cols, bins, _, _ = dims
    tiles = cols // SUBLANES
    if first:
        mask_t, owner_t, courant_ref, adv_ref, part_ref, grad_ref, flow_ref = refs[:7]
        mask_ref, owner_ref, e_here, o_here, sems = refs[7:]

        def e_copy(k):
            lanes = pl.ds(pl.multiple_of(k * LANES, LANES), LANES)
            return pltpu.make_async_copy(e_ref.at[..., lanes], e_here.at[k], sems.at[k])

        o_copy = pltpu.make_async_copy(o_ref, o_here, sems.at[bins // LANES])
        o_copy.start()
        for k in range(bins // LANES):
            e_copy(k).start()
        mask = mask_t[...].astype(F32)
        owner = owner_t[...]
        for i in range(tiles):
            for r in range(rows):
                for to_ref, values in ((mask_ref, mask), (owner_ref, owner)):
                    to_ref[i, span(r), :] = jnp.broadcast_to(
                        values[span(i), r : r + 1], (SUBLANES, LANES)
                    )
        o_copy.wait()
    else:
        mask_ref, courant_ref, adv_ref, part_ref, grad_ref, flow_ref = refs

    def arrived(k):
        if first:
            e_copy(k).wait()

    def energy_at(k, i, r):
        return e_here[k, r, i] if first else e_ref[k, i, span(r), :]

    def ocean_at(q, i, r):
        return o_here[q, r, i] if first else o_ref[q, i, span(r), :]

    for way in range(2):
        for i in range(tiles):
            for r in range(rows):
                flow_ref[way, i, span(r), :] = jnp.broadcast_to(
                    current_gain * ocean_at(way, i, r)[:, 0:1], (SUBLANES, LANES)
                )
    ocean_all(dims, ocean_at, mask_ref, part_ref, grad_ref)
    advect_all(dims, energy_at, arrived, flow_ref, mask_ref, courant_ref, adv_ref)


def fix_column(dims, parity, index, halo_ref, flow_ref, mask_ref, courant_ref, adv_ref):
    tile, spots = column_place(dims, parity, index)
    sign = side_sign(parity, index)
    sea = mask_ref[tile, spots, :]
    speed = flow_ref[0, tile, spots, :]
    for k in range(dims[2] // LANES):
        lanes = slice(k * LANES, (k + 1) * LANES)
        inward = jnp.maximum(sign * (courant_ref[0:1, lanes] + speed), 0.0)
        adv_ref[k, tile, spots, :] = (
            adv_ref[k, tile, spots, :] + sea * inward * halo_ref[:, lanes]
        )


def fix_row(dims, parity, index, halo_ref, flow_ref, mask_ref, courant_ref, adv_ref):
    spots = row_place(dims, parity, index)
    sign = side_sign(parity, index)
    for i in range(dims[1] // SUBLANES):
        sea = mask_ref[i, spots, :]
        speed = flow_ref[1, i, spots, :]
        for k in range(dims[2] // LANES):
            lanes = slice(k * LANES, (k + 1) * LANES)
            inward = jnp.maximum(sign * (courant_ref[1:2, lanes] + speed), 0.0)
            adv_ref[k, i, spots, :] = (
                adv_ref[k, i, spots, :] + sea * inward * halo_ref[i, :, lanes]
            )


def ocean_border(dims, sign, along, tile, spots, halo, mask_ref, drift_ref, out_ref):
    _, _, bins, levels, fields = dims
    sea = mask_ref[tile, spots, :]
    shear = (sign * (0.5 * transport)) * drift_ref[along, spots, :]
    for q in range(fields):
        value = halo(slice(bins + q * levels, bins + (q + 1) * levels))
        gain = mixing_side if q < 2 else mixing_side + shear
        out_ref[q, spots, :] = out_ref[q, spots, :] + sea * (gain * value)


def source_of(dims, mats, tile, adv_ref, owner_ref, m_ref):
    chunks = dims[2] // LANES
    owner = owner_ref[tile]
    low = jnp.concatenate(
        [
            jnp.where(owner == m, adv_ref[k, tile], 0.0).astype(BF16)
            for m in range(mats)
            for k in range(chunks)
        ],
        axis=1,
    )
    weights = jnp.concatenate([m_ref[m] for m in range(mats)], axis=1)
    return lax.dot_general(low, weights, (((1,), (1,)), ((), ())), preferred_element_type=F32)


def ocean_tile(dims, tile, col_border, row_borders, parity, part_ref, grad_ref, mask_ref,
               w_ref, low_ref, drift_ref, out_ref):
    _, _, _, levels, fields = dims
    drift = jnp.dot(low_ref[...], w_ref[...], preferred_element_type=F32)
    for k in range(2):
        drift_ref[k] = drift[:, k * levels : (k + 1) * levels]
    sea = mask_ref[tile]
    along = sea * drift[:, 0:levels]
    across = sea * drift[:, levels : 2 * levels]
    out_ref[0] = part_ref[0, tile] + rotation * across
    out_ref[1] = part_ref[1, tile] - rotation * along
    for q in range(2, fields):
        grad = along * grad_ref[2 * (q - 2), tile] + across * grad_ref[2 * (q - 2) + 1, tile]
        out_ref[q] = part_ref[q, tile] - (0.5 * transport) * grad
    if col_border is not None:
        index, halo_ref = col_border
        _, spots = column_place(dims, parity[0], index)
        ocean_border(
            dims, side_sign(parity[0], index), 0, tile, spots, lambda lanes: halo_ref[:, lanes],
            mask_ref, drift_ref, out_ref,
        )
    for index, halo_ref in enumerate(row_borders):
        ocean_border(
            dims, side_sign(parity[1], index), 1, tile, row_place(dims, parity[1], index),
            lambda lanes: halo_ref[tile, :, lanes], mask_ref, drift_ref, out_ref,
        )


def step_kernel(dims, mats, late, last, n_col, n_row, *refs):
    rows, cols, bins, levels, fields = dims
    tiles = cols // SUBLANES
    parity_ref, courant_ref, _, part_ref, grad_ref, flow_ref = refs[:6]
    mask_ref, owner_ref, m_ref, w_ref = refs[6:10]
    refs = refs[10:]
    got_col, got_row, refs = refs[0], refs[1 : 1 + n_row], refs[1 + n_row :]
    if late:
        e_early, o_early, *refs = refs
    adv_ref, e_out, o_out, *refs = refs
    if late and not last:
        col_refs, row_refs, refs = refs[:n_col], refs[n_col : n_col + n_row], refs[n_col + n_row :]
    low_ref, drift_ref, *refs = refs
    parity = parity_ref[0], parity_ref[1]
    index = 1 if late else 0
    walk = parity[0]
    todo = [walk * i + (1 - walk) * (tiles - 1 - i) for i in range(tiles)]
    copies = []
    if late and last:
        e_tile, o_tile, sems = refs

        def store(number, e_from, o_from):
            tile = todo[number]
            made = [pltpu.make_async_copy(e_from, e_out.at[:, tile], sems.at[number, 0])]
            for q in range(fields):
                made.append(
                    pltpu.make_async_copy(
                        o_from.at[q].reshape(rows, SUBLANES, levels),
                        o_out.at[q, :, tile],
                        sems.at[number, 1 + q],
                    )
                )
            return made

        for number in range(tiles - 1):
            copies += store(number, e_early.at[number], o_early.at[number])
        for copy in copies:
            copy.start()
    fixed = (flow_ref, mask_ref, courant_ref, adv_ref)
    if not late:
        for row_index in range(n_row):
            fix_row(dims, parity[1], row_index, got_row[row_index], *fixed)
    fix_column(dims, parity[0], index, got_col, *fixed)
    for number, tile in enumerate(todo):
        if late != (number == tiles - 1):
            continue
        source = source_of(dims, mats, tile, adv_ref, owner_ref, m_ref)
        sea = mask_ref[tile]
        for k in range(bins // LANES):
            lanes = slice(k * LANES, (k + 1) * LANES)
            energy = sea * (adv_ref[k, tile] + source_gain * source[:, lanes])
            if not last:
                e_out[k, tile] = energy
            elif late:
                e_tile[:, :, lanes] = energy.reshape(rows, SUBLANES, LANES)
            else:
                e_out[number, :, :, lanes] = energy.reshape(rows, SUBLANES, LANES)
            low_ref[:, lanes] = energy.astype(BF16)
        if not last:
            out_ref = o_out.at[:, tile]
        elif late:
            out_ref = o_tile
            e_copy, *o_copies = store(number, e_tile, o_tile)
            e_copy.start()
        else:
            out_ref = o_out.at[number]
        ocean_tile(
            dims, tile, (index, got_col) if late or number == 0 else None, got_row, parity,
            part_ref, grad_ref, mask_ref, w_ref, low_ref, drift_ref, out_ref,
        )
    if late and last:
        for copy in o_copies:
            copy.start()
        for copy in copies + [e_copy] + o_copies:
            copy.wait()
    elif late:

        def pack(to_ref, take):
            for k in lane_chunks(bins):
                to_ref[..., k : k + LANES] = take(e_out.at[k // LANES])
            for q in range(fields):
                to_ref[..., bins + q * levels : bins + (q + 1) * levels] = take(o_out.at[q])

        for i, to_ref in enumerate(col_refs):
            tile, spots = column_place(dims, parity[0], i)
            pack(to_ref, lambda ref: ref[tile, spots, :])
        for i, to_ref in enumerate(row_refs):
            spots = row_place(dims, parity[1], i)
            pack(to_ref, lambda ref: ref[:, spots, :])


def swap_pairs(values, axis):
    count = lax.axis_size(axis)
    got = []
    for index, value in enumerate(values):
        pairs = []
        for i in range(index, count - 1, 2):
            pairs += [(i, i + 1), (i + 1, i)]
        got.append(lax.ppermute(value, axis, pairs))
    return got


def local(spectrum, matrices, ownership, land_mask, courant, stokes_weight, ocean):
    bins, rows, cols = spectrum.shape
    fields, _, _, levels = ocean.shape
    mats = matrices.shape[2]
    tiles = cols // SUBLANES
    chunks = bins // LANES
    points_count = rows * cols
    dims = (rows, cols, bins, levels, fields)
    n_col = 2
    n_row = 2 if lax.axis_size("tile") > 2 else 1
    e0 = jnp.transpose(spectrum, (1, 2, 0)).reshape(rows, tiles, SUBLANES, bins)
    o0 = ocean.reshape(fields, rows, tiles, SUBLANES, levels)
    m0 = matrices.reshape(mats, bins, bins)
    mask_t = land_mask.T
    owner_t = ownership.T
    parity = jnp.stack([lax.axis_index("grp") % 2, lax.axis_index("tile") % 2]).astype(jnp.int32)

    vmem = pl.BlockSpec(memory_space=VMEM)
    smem = pl.BlockSpec(memory_space=pltpu.SMEM)
    hbm = pl.BlockSpec(memory_space=pltpu.HBM)

    def points(lead, width=LANES, dtype=F32):
        return VMEM((*lead, tiles, rows * SUBLANES, width), dtype)

    adv_shape = points((chunks,))
    o_shape = points((fields,), levels)
    window_shapes = [adv_shape, o_shape, points((2 * (fields - 2),), levels), points((2,))]
    wide = bins + fields * levels
    borders = [VMEM((rows, wide), F32)] * n_col + [VMEM((tiles, SUBLANES, wide), F32)] * n_row
    dma = pltpu.SemaphoreType.DMA
    moved = 4 * points_count * (chunks * LANES + fields * levels)
    cost = pl.CostEstimate(flops=0, transcendentals=0, bytes_accessed=4 * moved)

    def params(mib):
        return pltpu.CompilerParams(vmem_limit_bytes=mib * 2**20)

    def exchange(sent):
        return swap_pairs(sent[:n_col], "grp") + swap_pairs(sent[n_col:], "tile")

    sent = pl.pallas_call(
        functools.partial(first_kernel, dims, n_col, n_row),
        out_shape=borders,
        in_specs=[smem, hbm, hbm],
        out_specs=[vmem] * len(borders),
        scratch_shapes=[dma((n_col + n_row, 1 + fields))],
        compiler_params=params(8),
        cost_estimate=cost,
        name="first",
    )(parity, in_hbm(e0), in_hbm(o0))
    e = o = None
    for step in range(STEPS):
        got = exchange(sent)
        if step == 0:
            adv, part, grad, flow, mask, owner = pl.pallas_call(
                functools.partial(window_kernel, dims, True),
                out_shape=window_shapes + [points(()), points((), LANES, jnp.int32)],
                in_specs=[hbm] * 2 + [vmem] * 3,
                out_specs=[vmem] * 6,
                scratch_shapes=[
                    VMEM((chunks, rows, tiles, SUBLANES, LANES), F32),
                    VMEM((fields, rows, tiles, SUBLANES, levels), F32),
                    dma((chunks + 1,)),
                ],
                compiler_params=params(12),
                cost_estimate=cost,
                name="window_first",
            )(in_hbm(e0), in_hbm(o0), mask_t, owner_t, courant)
        else:
            adv, part, grad, flow = pl.pallas_call(
                functools.partial(window_kernel, dims, False),
                out_shape=window_shapes,
                in_specs=[vmem] * 4,
                out_specs=[vmem] * 4,
                compiler_params=params(8),
                cost_estimate=cost,
                name="window",
            )(e, o, mask, courant)
        last = step == STEPS - 1
        scratch = [VMEM((rows * SUBLANES, bins), BF16), VMEM((2, rows * SUBLANES, levels), F32)]
        if last:
            early_shape = [
                VMEM((tiles - 1, rows, SUBLANES, bins), F32),
                VMEM((tiles - 1, fields, rows * SUBLANES, levels), F32),
            ]
        else:
            early_shape = [adv_shape, o_shape]
        common = (mask, owner, m0, stokes_weight)
        adv, e, o = pl.pallas_call(
            functools.partial(step_kernel, dims, mats, False, last, n_col, n_row),
            out_shape=[adv_shape] + early_shape,
            in_specs=[smem] + [vmem] * (10 + n_row),
            out_specs=[vmem] * 3,
            scratch_shapes=scratch,
            input_output_aliases={2: 0},
            compiler_params=params(24),
            name="early_last" if last else "early",
        )(parity, courant, adv, part, grad, flow, *common, got[0], *got[n_col:])
        e_at = 11 + n_row
        aliases = {2: 0}
        if last:
            late_shape = [pltpu.HBM(e0.shape, F32), pltpu.HBM(o0.shape, F32)]
            late_specs = [vmem, hbm, hbm]
            scratch += [
                VMEM((rows, SUBLANES, bins), F32),
                VMEM((fields, rows * SUBLANES, levels), F32),
                dma((tiles, 1 + fields)),
            ]
        else:
            late_shape = early_shape + borders
            late_specs = [vmem] * (1 + len(late_shape))
            aliases.update({e_at: 1, e_at + 1: 2})
        _, e, o, *sent = pl.pallas_call(
            functools.partial(step_kernel, dims, mats, True, last, n_col, n_row),
            out_shape=[adv_shape] + late_shape,
            in_specs=[smem] + [vmem] * (12 + n_row),
            out_specs=late_specs,
            scratch_shapes=scratch,
            input_output_aliases=aliases,
            compiler_params=params(24),
            name="late_last" if last else "late",
        )(parity, courant, adv, part, grad, flow, *common, got[1], *got[n_col:], e, o)
    energy = jnp.transpose(e.reshape(rows, cols, bins), (2, 0, 1))
    return energy, o.reshape(ocean.shape)


def solution(mesh):
    in_specs = (
        P(None, "tile", "grp"),
        P("tile", "grp", None, None, None),
        P("tile", "grp"),
        P("tile", "grp"),
        P(),
        P(),
        P(None, "tile", "grp", None),
    )
    out_specs = (P(None, "tile", "grp"), P(None, "tile", "grp", None))
    return jax.shard_map(local, mesh=mesh, in_specs=in_specs, out_specs=out_specs, check_vma=False)
```

```python
import functools

import jax
import jax.numpy as jnp
from jax import lax
from jax.experimental import pallas as pl
from jax.experimental.pallas import tpu as pltpu
from jax.sharding import PartitionSpec as P


STEPS = 2

current_gain = 0.2
source_gain = 0.5
mixing_side = 0.15
mixing_depth = 0.2
rotation = 0.3
transport = 0.5

LANES = 128
SUBLANES = 8
BLOCK = 512
VMEM = pltpu.VMEM
F32 = jnp.float32
BF16 = jnp.bfloat16


def in_hbm(x):
    return pltpu.with_memory_space_constraint(x, pltpu.HBM)


def lane_chunks(width):
    return range(0, width, LANES)


def low_side(parity, index):
    return parity if index == 0 else 1 - parity


def column_place(dims, parity, index):
    rows, cols, _, _, _ = dims
    high = 1 - low_side(parity, index)
    tile = high * (cols // SUBLANES - 1)
    return tile, pl.ds(high * (SUBLANES - 1), rows, stride=SUBLANES)


def row_place(dims, parity, index):
    high = 1 - low_side(parity, index)
    return pl.ds(pl.multiple_of(high * (dims[0] - 1) * SUBLANES, SUBLANES), SUBLANES)


def side_sign(parity, index):
    return jnp.where(low_side(parity, index) == 1, 1.0, -1.0).astype(F32)


def first_kernel(dims, n_col, n_row, place_ref, e_hbm, o_hbm, *refs):
    rows, cols, bins, levels, fields = dims
    col_refs = refs[:n_col]
    row_refs = refs[n_col : n_col + n_row]
    e_all, o_all = refs[n_col + n_row : n_col + n_row + 2]
    sems, all_sems = refs[-2:]
    parity_ref = lax.rem(place_ref[0], 2), lax.rem(place_ref[1], 2)

    def pieces(to_ref, e_from, o_from, slot):
        copies = [pltpu.make_async_copy(e_from, to_ref.at[..., 0:bins], sems.at[slot, 0])]
        for q in range(fields):
            lanes = pl.ds(bins + q * levels, levels)
            copies.append(
                pltpu.make_async_copy(o_from(q), to_ref.at[..., lanes], sems.at[slot, 1 + q])
            )
        return copies

    def column(index, high):
        tile = high * (cols // SUBLANES - 1)
        place = high * (SUBLANES - 1)
        return pieces(
            col_refs[index],
            e_hbm.at[:, tile, place, :],
            lambda q: o_hbm.at[q, :, tile, place, :],
            index,
        )

    def row(index):
        r = (1 - low_side(parity_ref[1], index)) * (rows - 1)
        return pieces(row_refs[index], e_hbm.at[r], lambda q: o_hbm.at[q, r], n_col + index)

    for odd in range(2):

        @pl.when(parity_ref[0] == odd)
        def _(odd=odd):
            for index in reversed(range(n_col)):
                for copy in column(index, 1 - low_side(odd, index)):
                    copy.start()

    for index in range(n_row):
        for copy in row(index):
            copy.start()
    loads = [
        pltpu.make_async_copy(o_hbm, o_all, all_sems.at[0]),
        pltpu.make_async_copy(e_hbm, e_all, all_sems.at[1]),
    ]
    for copy in loads:
        copy.start()
    for copy in loads:
        copy.wait()
    for index in range(n_col):
        for copy in column(index, 0):
            copy.wait()
    for index in range(n_row):
        for copy in row(index):
            copy.wait()


def shifted(parts, axis_ids, ahead):
    first, final = axis_ids
    out = []
    if ahead:
        turned = [pltpu.roll(x, SUBLANES - 1, axis=0) for x in parts]
        for i, x in enumerate(turned):
            out.append(jnp.where(final, turned[i + 1] if i + 1 < len(parts) else 0.0, x))
    else:
        turned = [pltpu.roll(x, 1, axis=0) for x in parts]
        for i, x in enumerate(turned):
            out.append(jnp.where(first, turned[i - 1] if i else 0.0, x))
    return out


def sublane_ends():
    ids = lax.broadcasted_iota(jnp.int32, (SUBLANES, LANES), 0)
    return ids == 0, ids == SUBLANES - 1


def span(r):
    return slice(r * SUBLANES, (r + 1) * SUBLANES)


def advect_all(dims, energy_at, flow_ref, mask_ref, courant_ref, adv_ref):
    rows, cols, bins, _, _ = dims
    ends = sublane_ends()
    tiles = cols // SUBLANES

    def body(k, _):
        lanes = pl.ds(pl.multiple_of(k * LANES, LANES), LANES)
        speeds = [
            jnp.broadcast_to(courant_ref[way : way + 1, lanes], (SUBLANES, LANES))
            for way in range(2)
        ]

        def load(r):
            if r >= rows:
                return None
            return [energy_at(k, i, r) for i in range(tiles)]

        mid = load(0)
        falls = mid
        for r in range(rows):
            following = load(r + 1)
            if following is None:
                falls_next = [-x for x in mid]
            else:
                falls_next = [b - a for a, b in zip(mid, following)]
            west = shifted(mid, ends, False)
            east = shifted(mid, ends, True)
            for i in range(tiles):
                speed_x = speeds[0] + flow_ref[0, i, span(r), :]
                speed_y = speeds[1] + flow_ref[1, i, span(r), :]
                flux = speed_x * jnp.where(speed_x > 0, mid[i] - west[i], east[i] - mid[i])
                flux = flux + speed_y * jnp.where(speed_y > 0, falls[i], falls_next[i])
                adv_ref[k, i, span(r), :] = mask_ref[i, span(r), :] * (mid[i] - flux)
            mid, falls = following, falls_next
        return 0

    lax.fori_loop(0, bins // LANES, body, 0)


def ocean_all(dims, ocean_at, mask_ref, part_ref, grad_ref):
    rows, cols, _, levels, fields = dims
    ends = sublane_ends()
    level_id = lax.broadcasted_iota(jnp.int32, (SUBLANES, levels), 1)
    top = level_id == 0
    bottom = level_id == levels - 1
    tiles = cols // SUBLANES

    for q in range(fields):
        north = None
        mid = [ocean_at(q, i, 0) for i in range(tiles)]
        for r in range(rows):
            south = None
            if r + 1 < rows:
                south = [ocean_at(q, i, r + 1) for i in range(tiles)]
            west = shifted(mid, ends, False)
            east = shifted(mid, ends, True)
            for i in range(tiles):
                own = mid[i]
                if north is None:
                    across, slope = south[i], south[i]
                elif south is None:
                    across, slope = north[i], -north[i]
                else:
                    across, slope = north[i] + south[i], south[i] - north[i]
                above = jnp.where(top, 0.0, pltpu.roll(own, 1, axis=1))
                below = jnp.where(bottom, 0.0, pltpu.roll(own, levels - 1, axis=1))
                tend = mixing_side * (across + (west[i] + east[i])) + mixing_depth * (above + below)
                tend = tend - (4 * mixing_side + 2 * mixing_depth) * own
                if q == 0:
                    tend = tend + rotation * ocean_at(1, i, r)
                elif q == 1:
                    tend = tend - rotation * ocean_at(0, i, r)
                else:
                    grad_ref[2 * (q - 2), i, span(r), :] = east[i] - west[i]
                    grad_ref[2 * (q - 2) + 1, i, span(r), :] = slope
                part_ref[q, i, span(r), :] = own + mask_ref[i, span(r), :] * tend
            north, mid = mid, south


def window_kernel(dims, first, e_ref, o_ref, *refs):
    rows, cols, _, _, _ = dims
    tiles = cols // SUBLANES
    if first:
        mask_t, owner_t, courant_ref, m_hbm, w_hbm, adv_ref, part_ref, grad_ref, flow_ref = refs[:9]
        mask_ref, owner_ref, m_ref, w_ref, sems = refs[9:]
        copies = [
            pltpu.make_async_copy(m_hbm, m_ref, sems.at[0]),
            pltpu.make_async_copy(w_hbm, w_ref, sems.at[1]),
        ]
        for copy in copies:
            copy.start()
        mask = mask_t[...].astype(F32)
        owner = owner_t[...]
        for i in range(tiles):
            for r in range(rows):
                for to_ref, values in ((mask_ref, mask), (owner_ref, owner)):
                    to_ref[i, span(r), :] = jnp.broadcast_to(
                        values[span(i), r : r + 1], (SUBLANES, LANES)
                    )
    else:
        mask_ref, courant_ref, adv_ref, part_ref, grad_ref, flow_ref = refs
        copies = []

    def energy_at(k, i, r):
        if first:
            return e_ref[r, i, :, pl.ds(pl.multiple_of(k * LANES, LANES), LANES)]
        return e_ref[k, i, span(r), :]

    def ocean_at(q, i, r):
        return o_ref[q, r, i] if first else o_ref[q, i, span(r), :]

    for way in range(2):
        for i in range(tiles):
            for r in range(rows):
                flow_ref[way, i, span(r), :] = jnp.broadcast_to(
                    current_gain * ocean_at(way, i, r)[:, 0:1], (SUBLANES, LANES)
                )
    ocean_all(dims, ocean_at, mask_ref, part_ref, grad_ref)
    advect_all(dims, energy_at, flow_ref, mask_ref, courant_ref, adv_ref)
    for copy in copies:
        copy.wait()


def real(spot, index):
    place, count = spot
    if index == 0 and count % 2 == 0:
        return None
    low = low_side(lax.rem(place, 2), index)
    partner = place + 1 - 2 * low
    return jnp.logical_and(partner >= 0, partner < count)


def kept(valid, value):
    return value if valid is None else jnp.where(valid, value, 0.0)


def fix_column(dims, parity, index, valid, halo_ref, flow_ref, mask_ref, courant_ref, adv_ref):
    tile, spots = column_place(dims, parity, index)
    sign = side_sign(parity, index)
    sea = mask_ref[tile, spots, :]
    speed = flow_ref[0, tile, spots, :]
    for k in range(dims[2] // LANES):
        lanes = slice(k * LANES, (k + 1) * LANES)
        inward = jnp.maximum(sign * (courant_ref[0:1, lanes] + speed), 0.0)
        adv_ref[k, tile, spots, :] = (
            adv_ref[k, tile, spots, :] + sea * inward * kept(valid, halo_ref[:, lanes])
        )


def fix_row(dims, parity, index, valid, halo_ref, flow_ref, mask_ref, courant_ref, adv_ref):
    spots = row_place(dims, parity, index)
    sign = side_sign(parity, index)
    for i in range(dims[1] // SUBLANES):
        sea = mask_ref[i, spots, :]
        speed = flow_ref[1, i, spots, :]
        for k in range(dims[2] // LANES):
            lanes = slice(k * LANES, (k + 1) * LANES)
            inward = jnp.maximum(sign * (courant_ref[1:2, lanes] + speed), 0.0)
            adv_ref[k, i, spots, :] = (
                adv_ref[k, i, spots, :] + sea * inward * kept(valid, halo_ref[i, :, lanes])
            )


def ocean_border(dims, sign, along, tile, spots, halo, mask_ref, drift_ref, out_ref):
    _, _, bins, levels, fields = dims
    sea = mask_ref[tile, spots, :]
    shear = (sign * (0.5 * transport)) * drift_ref[along, spots, :]
    for q in range(fields):
        value = halo(slice(bins + q * levels, bins + (q + 1) * levels))
        gain = mixing_side if q < 2 else mixing_side + shear
        out_ref[q, spots, :] = out_ref[q, spots, :] + sea * (gain * value)


def low_of(dims, mats, tile, adv_ref, owner_ref):
    owner = owner_ref[tile]
    return jnp.concatenate(
        [
            jnp.where(owner == m, adv_ref[k, tile], 0.0).astype(BF16)
            for m in range(mats)
            for k in range(dims[2] // LANES)
        ],
        axis=1,
    )


def source_of(mats, low, m_ref, begin, end):
    weights = jnp.concatenate([m_ref[m, begin:end, :] for m in range(mats)], axis=1)
    return lax.dot_general(low, weights, (((1,), (1,)), ((), ())), preferred_element_type=F32)


def ocean_tile(dims, tile, col_border, row_borders, parity, part_ref, grad_ref, mask_ref,
               w_ref, low_ref, drift_ref, out_ref):
    _, _, _, levels, fields = dims
    drift = jnp.dot(low_ref[...], w_ref[...], preferred_element_type=F32)
    for k in range(2):
        drift_ref[k] = drift[:, k * levels : (k + 1) * levels]
    sea = mask_ref[tile]
    along = sea * drift[:, 0:levels]
    across = sea * drift[:, levels : 2 * levels]
    out_ref[0] = part_ref[0, tile] + rotation * across
    out_ref[1] = part_ref[1, tile] - rotation * along
    for q in range(2, fields):
        grad = along * grad_ref[2 * (q - 2), tile] + across * grad_ref[2 * (q - 2) + 1, tile]
        out_ref[q] = part_ref[q, tile] - (0.5 * transport) * grad
    if col_border is not None:
        index, valid, col_ref = col_border
        _, spots = column_place(dims, parity[0], index)
        ocean_border(
            dims, side_sign(parity[0], index), 0, tile, spots,
            lambda lanes: kept(valid, col_ref[:, lanes]), mask_ref, drift_ref, out_ref,
        )
    for index, (valid, row_ref) in enumerate(row_borders):
        ocean_border(
            dims, side_sign(parity[1], index), 1, tile, row_place(dims, parity[1], index),
            lambda lanes: kept(valid, row_ref[tile, :, lanes]), mask_ref, drift_ref, out_ref,
        )


def step_kernel(dims, mats, counts, late, last, n_col, n_row, *refs):
    rows, cols, bins, levels, fields = dims
    tiles = cols // SUBLANES
    place_ref, courant_ref, _, part_ref, grad_ref, flow_ref = refs[:6]
    mask_ref, owner_ref, m_ref, w_ref = refs[6:10]
    refs = refs[10:]
    got_col, got_row, refs = refs[0], refs[1 : 1 + n_row], refs[1 + n_row :]
    if late:
        e_early, o_early, *refs = refs
    adv_ref, e_out, o_out, *refs = refs
    if late and not last:
        col_refs, row_refs, refs = refs[:n_col], refs[n_col : n_col + n_row], refs[n_col + n_row :]
    low_ref, drift_ref, *refs = refs
    parity = lax.rem(place_ref[0], 2), lax.rem(place_ref[1], 2)
    index = 1 if late else 0
    col_valid = real((place_ref[0], counts[0]), index)
    row_valid = [real((place_ref[1], counts[1]), i) for i in range(n_row)]
    walk = parity[0]
    todo = [walk * i + (1 - walk) * (tiles - 1 - i) for i in range(tiles)]
    copies = []
    if late and last:
        e_tile, o_tile, sems = refs

        def store(number, e_from, o_from):
            tile = todo[number]
            made = [pltpu.make_async_copy(e_from, e_out.at[:, tile], sems.at[number, 0])]
            for q in range(fields):
                made.append(
                    pltpu.make_async_copy(
                        o_from.at[q].reshape(rows, SUBLANES, levels),
                        o_out.at[q, :, tile],
                        sems.at[number, 1 + q],
                    )
                )
            return made

        for number in range(tiles - 1):
            copies += store(number, e_early.at[number], o_early.at[number])
        for copy in copies:
            copy.start()
    fixed = (flow_ref, mask_ref, courant_ref, adv_ref)
    if not late:
        for row_index in range(n_row):
            fix_row(
                dims, parity[1], row_index, row_valid[row_index], got_row[row_index], *fixed
            )
    fix_column(dims, parity[0], index, col_valid, got_col, *fixed)
    for number, tile in enumerate(todo):
        if late != (number == tiles - 1):
            continue
        low = low_of(dims, mats, tile, adv_ref, owner_ref)
        sea = mask_ref[tile]
        for k in range(bins // LANES):
            lanes = slice(k * LANES, (k + 1) * LANES)
            begin = k * LANES // BLOCK * BLOCK
            if k * LANES == begin:
                source = source_of(mats, low, m_ref, begin, min(begin + BLOCK, bins))
            gain = source[:, k * LANES - begin : (k + 1) * LANES - begin]
            energy = sea * (adv_ref[k, tile] + source_gain * gain)
            if not last:
                e_out[k, tile] = energy
            elif late:
                e_tile[:, :, lanes] = energy.reshape(rows, SUBLANES, LANES)
            else:
                e_out[number, :, :, lanes] = energy.reshape(rows, SUBLANES, LANES)
            low_ref[:, lanes] = energy.astype(BF16)
        if not last:
            out_ref = o_out.at[:, tile]
        elif late:
            out_ref = o_tile
            e_copy, *o_copies = store(number, e_tile, o_tile)
            e_copy.start()
        else:
            out_ref = o_out.at[number]
        ocean_tile(
            dims, tile, (index, col_valid, got_col) if late or number == 0 else None,
            list(zip(row_valid, got_row)), parity,
            part_ref, grad_ref, mask_ref, w_ref, low_ref, drift_ref, out_ref,
        )
    if late and last:
        for copy in o_copies:
            copy.start()
        for copy in copies + [e_copy] + o_copies:
            copy.wait()
    elif late:

        def pack(to_ref, take):
            for k in lane_chunks(bins):
                to_ref[..., k : k + LANES] = take(e_out.at[k // LANES])
            for q in range(fields):
                to_ref[..., bins + q * levels : bins + (q + 1) * levels] = take(o_out.at[q])

        for i, to_ref in enumerate(col_refs):
            tile, spots = column_place(dims, parity[0], i)
            pack(to_ref, lambda ref: ref[tile, spots, :])
        for i, to_ref in enumerate(row_refs):
            spots = row_place(dims, parity[1], i)
            pack(to_ref, lambda ref: ref[:, spots, :])


def swap_pairs(values, axis, other):
    size = {name: lax.axis_size(name) for name in (axis, other)}
    names = ("grp", "tile")

    def device(along, across):
        spot = {axis: along, other: across}
        return spot[names[0]] * lax.axis_size(names[1]) + spot[names[1]]

    got = []
    for index, value in enumerate(values):
        pairs = []
        for i in range(size[axis]):
            partner = i + 1 if (i - index) % 2 == 0 else i - 1
            for j in range(size[other]):
                if 0 <= partner < size[axis]:
                    pairs.append((device(i, j), device(partner, j)))
                elif j ^ 1 < size[other]:
                    pairs.append((device(i, j), device(i, j ^ 1)))
        got.append(lax.ppermute(value, names, pairs))
    return got


def local(spectrum, matrices, ownership, land_mask, courant, stokes_weight, ocean):
    bins, rows, cols = spectrum.shape
    fields, _, _, levels = ocean.shape
    mats = matrices.shape[2]
    tiles = cols // SUBLANES
    chunks = bins // LANES
    dims = (rows, cols, bins, levels, fields)
    n_col = 2
    n_row = 2 if lax.axis_size("tile") > 2 else 1
    e0 = jnp.transpose(spectrum, (1, 2, 0)).reshape(rows, tiles, SUBLANES, bins)
    o0 = ocean.reshape(fields, rows, tiles, SUBLANES, levels)
    m0 = matrices.reshape(mats, bins, bins)
    mask_t = land_mask.T
    owner_t = ownership.T
    place = jnp.stack([lax.axis_index("grp"), lax.axis_index("tile")])
    counts = lax.axis_size("grp"), lax.axis_size("tile")

    vmem = pl.BlockSpec(memory_space=VMEM)
    smem = pl.BlockSpec(memory_space=pltpu.SMEM)
    hbm = pl.BlockSpec(memory_space=pltpu.HBM)

    def points(lead, width=LANES, dtype=F32):
        return VMEM((*lead, tiles, rows * SUBLANES, width), dtype)

    adv_shape = points((chunks,))
    o_shape = points((fields,), levels)
    window_shapes = [adv_shape, o_shape, points((2 * (fields - 2),), levels), points((2,))]
    wide = bins + fields * levels
    borders = [VMEM((rows, wide), F32)] * n_col + [VMEM((tiles, SUBLANES, wide), F32)] * n_row
    dma = pltpu.SemaphoreType.DMA

    def params(mib):
        return pltpu.CompilerParams(vmem_limit_bytes=mib * 2**20)

    def exchange(sent):
        return swap_pairs(sent[:n_col], "grp", "tile") + swap_pairs(sent[n_col:], "tile", "grp")

    sent = pl.pallas_call(
        functools.partial(first_kernel, dims, n_col, n_row),
        out_shape=borders + [VMEM(e0.shape, F32), VMEM(o0.shape, F32)],
        in_specs=[smem, hbm, hbm],
        out_specs=[vmem] * (len(borders) + 2),
        scratch_shapes=[dma((n_col + n_row, 1 + fields)), dma((2,))],
        compiler_params=params(8),
        name="first",
    )(place, in_hbm(e0), in_hbm(o0))
    e, o = sent[-2:]
    sent = sent[:-2]
    for step in range(STEPS):
        got = exchange(sent)
        if step == 0:
            adv, part, grad, flow, mask, owner, m, w = pl.pallas_call(
                functools.partial(window_kernel, dims, True),
                out_shape=window_shapes
                + [
                    points(()),
                    points((), LANES, jnp.int32),
                    VMEM(m0.shape, BF16),
                    VMEM(stokes_weight.shape, BF16),
                ],
                in_specs=[vmem] * 5 + [hbm] * 2,
                out_specs=[vmem] * 8,
                scratch_shapes=[dma((2,))],
                compiler_params=params(8),
                name="window_first",
            )(e, o, mask_t, owner_t, courant, in_hbm(m0), in_hbm(stokes_weight))
        else:
            adv, part, grad, flow = pl.pallas_call(
                functools.partial(window_kernel, dims, False),
                out_shape=window_shapes,
                in_specs=[vmem] * 4,
                out_specs=[vmem] * 4,
                compiler_params=params(8),
                name="window",
            )(e, o, mask, courant)
        last = step == STEPS - 1
        scratch = [VMEM((rows * SUBLANES, bins), BF16), VMEM((2, rows * SUBLANES, levels), F32)]
        if last:
            early_shape = [
                VMEM((tiles - 1, rows, SUBLANES, bins), F32),
                VMEM((tiles - 1, fields, rows * SUBLANES, levels), F32),
            ]
        else:
            early_shape = [adv_shape, o_shape]
        common = (mask, owner, m, w)
        adv, e, o = pl.pallas_call(
            functools.partial(step_kernel, dims, mats, counts, False, last, n_col, n_row),
            out_shape=[adv_shape] + early_shape,
            in_specs=[smem] + [vmem] * (10 + n_row),
            out_specs=[vmem] * 3,
            scratch_shapes=scratch,
            input_output_aliases={2: 0},
            compiler_params=params(24),
            name="early_last" if last else "early",
        )(place, courant, adv, part, grad, flow, *common, got[0], *got[n_col:])
        e_at = 11 + n_row
        aliases = {2: 0}
        if last:
            late_shape = [pltpu.HBM(e0.shape, F32), pltpu.HBM(o0.shape, F32)]
            late_specs = [vmem, hbm, hbm]
            scratch += [
                VMEM((rows, SUBLANES, bins), F32),
                VMEM((fields, rows * SUBLANES, levels), F32),
                dma((tiles, 1 + fields)),
            ]
        else:
            late_shape = early_shape + borders
            late_specs = [vmem] * (1 + len(late_shape))
            aliases.update({e_at: 1, e_at + 1: 2})
        _, e, o, *sent = pl.pallas_call(
            functools.partial(step_kernel, dims, mats, counts, True, last, n_col, n_row),
            out_shape=[adv_shape] + late_shape,
            in_specs=[smem] + [vmem] * (12 + n_row),
            out_specs=late_specs,
            scratch_shapes=scratch,
            input_output_aliases=aliases,
            compiler_params=params(24),
            name="late_last" if last else "late",
        )(place, courant, adv, part, grad, flow, *common, got[1], *got[n_col:], e, o)
    energy = jnp.transpose(e.reshape(rows, cols, bins), (2, 0, 1))
    return energy, o.reshape(ocean.shape)


def solution(mesh):
    in_specs = (
        P(None, "tile", "grp"),
        P("tile", "grp", None, None, None),
        P("tile", "grp"),
        P("tile", "grp"),
        P(),
        P(),
        P(None, "tile", "grp", None),
    )
    out_specs = (P(None, "tile", "grp"), P(None, "tile", "grp", None))
    return jax.shard_map(local, mesh=mesh, in_specs=in_specs, out_specs=out_specs, check_vma=False)
```

```python
import functools

import jax
import jax.numpy as jnp
from jax import lax
from jax.experimental import pallas as pl
from jax.experimental.pallas import tpu as pltpu
from jax.sharding import PartitionSpec as P


STEPS = 2

current_gain = 0.2
source_gain = 0.5
mixing_side = 0.15
mixing_depth = 0.2
rotation = 0.3
transport = 0.5

LANES = 128
SUBLANES = 8
BLOCK = 512
VMEM = pltpu.VMEM
F32 = jnp.float32
BF16 = jnp.bfloat16


def in_hbm(x):
    return pltpu.with_memory_space_constraint(x, pltpu.HBM)


def lane_chunks(width):
    return range(0, width, LANES)


def low_side(parity, index):
    return parity if index == 0 else 1 - parity


def column_place(dims, parity, index):
    rows, cols, _, _, _ = dims
    high = 1 - low_side(parity, index)
    tile = high * (cols // SUBLANES - 1)
    return tile, pl.ds(high * (SUBLANES - 1), rows, stride=SUBLANES)


def row_place(dims, parity, index):
    high = 1 - low_side(parity, index)
    return pl.ds(pl.multiple_of(high * (dims[0] - 1) * SUBLANES, SUBLANES), SUBLANES)


def side_sign(parity, index):
    return jnp.where(low_side(parity, index) == 1, 1.0, -1.0).astype(F32)


def spot():
    return lax.axis_index("grp"), lax.axis_index("tile")


def parities():
    return tuple(lax.rem(i, 2) for i in spot())


def first_kernel(dims, n_col, n_row, e_hbm, o_hbm, *refs):
    rows, cols, bins, levels, fields = dims
    chunks = bins // LANES
    col_refs = refs[:n_col]
    row_refs = refs[n_col : n_col + n_row]
    e_ref, o_ref, sems = refs[n_col + n_row :]
    loads = [
        pltpu.make_async_copy(e_hbm.at[:, pl.ds(k * LANES, LANES)], e_ref.at[k], sems.at[k])
        for k in range(chunks)
    ]
    loads.append(pltpu.make_async_copy(o_hbm, o_ref, sems.at[chunks]))
    for copy in loads:
        copy.start()
    parity = parities()

    def pack(lanes, ref):
        for i, to_ref in enumerate(col_refs):
            high = 1 - low_side(parity[0], i)
            to_ref[:, lanes] = ref[pl.ds(high * (cols - 1), rows, stride=cols), :]
        for i, to_ref in enumerate(row_refs):
            high = 1 - low_side(parity[1], i)
            begin = pl.multiple_of(high * (rows - 1) * cols, cols)
            to_ref[:, :, lanes] = ref[pl.ds(begin, cols), :].reshape(-1, SUBLANES, LANES)

    for k in range(chunks):
        loads[k].wait()
        pack(slice(k * LANES, (k + 1) * LANES), e_ref.at[k])
    loads[chunks].wait()
    for q in range(fields):
        pack(slice(bins + q * levels, bins + (q + 1) * levels), o_ref.at[q])


def shifted(parts, axis_ids, ahead):
    first, final = axis_ids
    out = []
    if ahead:
        turned = [pltpu.roll(x, SUBLANES - 1, axis=0) for x in parts]
        for i, x in enumerate(turned):
            out.append(jnp.where(final, turned[i + 1] if i + 1 < len(parts) else 0.0, x))
    else:
        turned = [pltpu.roll(x, 1, axis=0) for x in parts]
        for i, x in enumerate(turned):
            out.append(jnp.where(first, turned[i - 1] if i else 0.0, x))
    return out


def sublane_ends():
    ids = lax.broadcasted_iota(jnp.int32, (SUBLANES, LANES), 0)
    return ids == 0, ids == SUBLANES - 1


def span(r):
    return slice(r * SUBLANES, (r + 1) * SUBLANES)


def advect_all(dims, energy_at, flow_ref, mask_ref, courant_ref, adv_ref):
    rows, cols, bins, _, _ = dims
    ends = sublane_ends()
    tiles = cols // SUBLANES

    def body(k, _):
        lanes = pl.ds(pl.multiple_of(k * LANES, LANES), LANES)
        speeds = [
            jnp.broadcast_to(courant_ref[way : way + 1, lanes], (SUBLANES, LANES))
            for way in range(2)
        ]

        def load(r):
            if r >= rows:
                return None
            return [energy_at(k, i, r) for i in range(tiles)]

        mid = load(0)
        falls = mid
        for r in range(rows):
            following = load(r + 1)
            if following is None:
                falls_next = [-x for x in mid]
            else:
                falls_next = [b - a for a, b in zip(mid, following)]
            west = shifted(mid, ends, False)
            east = shifted(mid, ends, True)
            for i in range(tiles):
                speed_x = speeds[0] + flow_ref[0, i, span(r), :]
                speed_y = speeds[1] + flow_ref[1, i, span(r), :]
                flux = speed_x * jnp.where(speed_x > 0, mid[i] - west[i], east[i] - mid[i])
                flux = flux + speed_y * jnp.where(speed_y > 0, falls[i], falls_next[i])
                adv_ref[k, i, span(r), :] = mask_ref[i, span(r), :] * (mid[i] - flux)
            mid, falls = following, falls_next
        return 0

    lax.fori_loop(0, bins // LANES, body, 0)


def ocean_all(dims, ocean_at, mask_ref, part_ref, grad_ref):
    rows, cols, _, levels, fields = dims
    ends = sublane_ends()
    level_id = lax.broadcasted_iota(jnp.int32, (SUBLANES, levels), 1)
    top = level_id == 0
    bottom = level_id == levels - 1
    tiles = cols // SUBLANES

    for q in range(fields):
        north = None
        mid = [ocean_at(q, i, 0) for i in range(tiles)]
        for r in range(rows):
            south = None
            if r + 1 < rows:
                south = [ocean_at(q, i, r + 1) for i in range(tiles)]
            west = shifted(mid, ends, False)
            east = shifted(mid, ends, True)
            for i in range(tiles):
                own = mid[i]
                if north is None:
                    across, slope = south[i], south[i]
                elif south is None:
                    across, slope = north[i], -north[i]
                else:
                    across, slope = north[i] + south[i], south[i] - north[i]
                above = jnp.where(top, 0.0, pltpu.roll(own, 1, axis=1))
                below = jnp.where(bottom, 0.0, pltpu.roll(own, levels - 1, axis=1))
                tend = mixing_side * (across + (west[i] + east[i])) + mixing_depth * (above + below)
                tend = tend - (4 * mixing_side + 2 * mixing_depth) * own
                if q == 0:
                    tend = tend + rotation * ocean_at(1, i, r)
                elif q == 1:
                    tend = tend - rotation * ocean_at(0, i, r)
                else:
                    grad_ref[2 * (q - 2), i, span(r), :] = east[i] - west[i]
                    grad_ref[2 * (q - 2) + 1, i, span(r), :] = slope
                part_ref[q, i, span(r), :] = own + mask_ref[i, span(r), :] * tend
            north, mid = mid, south


def window_kernel(dims, first, e_ref, o_ref, *refs):
    rows, cols, _, _, _ = dims
    tiles = cols // SUBLANES
    if first:
        mask_t, owner_t, courant_ref, m_hbm, w_hbm, adv_ref, part_ref, grad_ref, flow_ref = refs[:9]
        mask_ref, owner_ref, m_ref, w_ref, sems = refs[9:]
        copies = [
            pltpu.make_async_copy(m_hbm, m_ref, sems.at[0]),
            pltpu.make_async_copy(w_hbm, w_ref, sems.at[1]),
        ]
        for copy in copies:
            copy.start()
        mask = mask_t[...].astype(F32)
        owner = owner_t[...]
        for i in range(tiles):
            for r in range(rows):
                for to_ref, values in ((mask_ref, mask), (owner_ref, owner)):
                    to_ref[i, span(r), :] = jnp.broadcast_to(
                        values[span(i), r : r + 1], (SUBLANES, LANES)
                    )
    else:
        mask_ref, courant_ref, adv_ref, part_ref, grad_ref, flow_ref = refs
        copies = []

    def energy_at(k, i, r):
        return e_ref[k, span(r * tiles + i), :] if first else e_ref[k, i, span(r), :]

    def ocean_at(q, i, r):
        return o_ref[q, span(r * tiles + i), :] if first else o_ref[q, i, span(r), :]

    for way in range(2):
        for i in range(tiles):
            for r in range(rows):
                flow_ref[way, i, span(r), :] = jnp.broadcast_to(
                    current_gain * ocean_at(way, i, r)[:, 0:1], (SUBLANES, LANES)
                )
    ocean_all(dims, ocean_at, mask_ref, part_ref, grad_ref)
    advect_all(dims, energy_at, flow_ref, mask_ref, courant_ref, adv_ref)
    for copy in copies:
        copy.wait()


def real(spot, index):
    place, count = spot
    if index == 0 and count % 2 == 0:
        return None
    low = low_side(lax.rem(place, 2), index)
    partner = place + 1 - 2 * low
    return jnp.logical_and(partner >= 0, partner < count)


def kept(valid, value):
    return value if valid is None else jnp.where(valid, value, 0.0)


def fix_column(dims, parity, index, valid, halo_ref, flow_ref, mask_ref, courant_ref, adv_ref):
    tile, spots = column_place(dims, parity, index)
    sign = side_sign(parity, index)
    sea = mask_ref[tile, spots, :]
    speed = flow_ref[0, tile, spots, :]
    for k in range(dims[2] // LANES):
        lanes = slice(k * LANES, (k + 1) * LANES)
        inward = jnp.maximum(sign * (courant_ref[0:1, lanes] + speed), 0.0)
        adv_ref[k, tile, spots, :] = (
            adv_ref[k, tile, spots, :] + sea * inward * kept(valid, halo_ref[:, lanes])
        )


def fix_row(dims, parity, index, valid, halo_ref, flow_ref, mask_ref, courant_ref, adv_ref):
    spots = row_place(dims, parity, index)
    sign = side_sign(parity, index)
    for i in range(dims[1] // SUBLANES):
        sea = mask_ref[i, spots, :]
        speed = flow_ref[1, i, spots, :]
        for k in range(dims[2] // LANES):
            lanes = slice(k * LANES, (k + 1) * LANES)
            inward = jnp.maximum(sign * (courant_ref[1:2, lanes] + speed), 0.0)
            adv_ref[k, i, spots, :] = (
                adv_ref[k, i, spots, :] + sea * inward * kept(valid, halo_ref[i, :, lanes])
            )


def ocean_border(dims, sign, along, tile, spots, halo, mask_ref, drift_ref, out_ref):
    _, _, bins, levels, fields = dims
    sea = mask_ref[tile, spots, :]
    shear = (sign * (0.5 * transport)) * drift_ref[along, spots, :]
    for q in range(fields):
        value = halo(slice(bins + q * levels, bins + (q + 1) * levels))
        gain = mixing_side if q < 2 else mixing_side + shear
        out_ref[q, spots, :] = out_ref[q, spots, :] + sea * (gain * value)


def low_of(dims, mats, tile, adv_ref, owner_ref):
    owner = owner_ref[tile]
    return jnp.concatenate(
        [
            jnp.where(owner == m, adv_ref[k, tile], 0.0).astype(BF16)
            for m in range(mats)
            for k in range(dims[2] // LANES)
        ],
        axis=1,
    )


def source_of(mats, low, m_ref, begin, end):
    weights = jnp.concatenate([m_ref[m, begin:end, :] for m in range(mats)], axis=1)
    return lax.dot_general(low, weights, (((1,), (1,)), ((), ())), preferred_element_type=F32)


def ocean_tile(dims, tile, col_border, row_borders, parity, part_ref, grad_ref, mask_ref,
               w_ref, low_ref, drift_ref, out_ref):
    _, _, _, levels, fields = dims
    drift = jnp.dot(low_ref[...], w_ref[...], preferred_element_type=F32)
    for k in range(2):
        drift_ref[k] = drift[:, k * levels : (k + 1) * levels]
    sea = mask_ref[tile]
    along = sea * drift[:, 0:levels]
    across = sea * drift[:, levels : 2 * levels]
    out_ref[0] = part_ref[0, tile] + rotation * across
    out_ref[1] = part_ref[1, tile] - rotation * along
    for q in range(2, fields):
        grad = along * grad_ref[2 * (q - 2), tile] + across * grad_ref[2 * (q - 2) + 1, tile]
        out_ref[q] = part_ref[q, tile] - (0.5 * transport) * grad
    if col_border is not None:
        index, valid, col_ref = col_border
        _, spots = column_place(dims, parity[0], index)
        ocean_border(
            dims, side_sign(parity[0], index), 0, tile, spots,
            lambda lanes: kept(valid, col_ref[:, lanes]), mask_ref, drift_ref, out_ref,
        )
    for index, (valid, row_ref) in enumerate(row_borders):
        ocean_border(
            dims, side_sign(parity[1], index), 1, tile, row_place(dims, parity[1], index),
            lambda lanes: kept(valid, row_ref[tile, :, lanes]), mask_ref, drift_ref, out_ref,
        )


def step_kernel(dims, mats, counts, late, last, n_col, n_row, *refs):
    rows, cols, bins, levels, fields = dims
    tiles = cols // SUBLANES
    courant_ref, _, part_ref, grad_ref, flow_ref = refs[:5]
    mask_ref, owner_ref, m_ref, w_ref = refs[5:9]
    refs = refs[9:]
    got_col, got_row, refs = refs[0], refs[1 : 1 + n_row], refs[1 + n_row :]
    if late:
        e_early, o_early, *refs = refs
    adv_ref, e_out, o_out, *refs = refs
    if late and not last:
        col_refs, row_refs, refs = refs[:n_col], refs[n_col : n_col + n_row], refs[n_col + n_row :]
    low_ref, drift_ref, *refs = refs
    here, parity = spot(), parities()
    index = 1 if late else 0
    col_valid = real((here[0], counts[0]), index)
    row_valid = [real((here[1], counts[1]), i) for i in range(n_row)]
    walk = parity[0]
    todo = [walk * i + (1 - walk) * (tiles - 1 - i) for i in range(tiles)]
    copies = []
    if late and last:
        e_tile, o_tile, sems = refs

        def store(number, e_from, o_from):
            tile = todo[number]
            made = []
            for begin in range(0, bins, BLOCK):
                lanes = pl.ds(begin, min(BLOCK, bins - begin))
                made.append(
                    pltpu.make_async_copy(
                        e_from.at[:, :, lanes],
                        e_out.at[:, tile, :, lanes],
                        sems.at[number, fields + begin // BLOCK],
                    )
                )
            for q in range(fields):
                made.append(
                    pltpu.make_async_copy(
                        o_from.at[q].reshape(rows, SUBLANES, levels),
                        o_out.at[q, :, tile],
                        sems.at[number, q],
                    )
                )
            return made

        for number in range(tiles - 1):
            copies += store(number, e_early.at[number], o_early.at[number])
        for copy in copies:
            copy.start()
    fixed = (flow_ref, mask_ref, courant_ref, adv_ref)
    if not late:
        for row_index in range(n_row):
            fix_row(
                dims, parity[1], row_index, row_valid[row_index], got_row[row_index], *fixed
            )
    fix_column(dims, parity[0], index, col_valid, got_col, *fixed)
    for number, tile in enumerate(todo):
        if late != (number == tiles - 1):
            continue
        low = low_of(dims, mats, tile, adv_ref, owner_ref)
        sea = mask_ref[tile]
        own_copies = store(number, e_tile, o_tile) if late and last else None
        for k in range(bins // LANES):
            lanes = slice(k * LANES, (k + 1) * LANES)
            begin = k * LANES // BLOCK * BLOCK
            if k * LANES == begin:
                source = source_of(mats, low, m_ref, begin, min(begin + BLOCK, bins))
            gain = source[:, k * LANES - begin : (k + 1) * LANES - begin]
            energy = sea * (adv_ref[k, tile] + source_gain * gain)
            if not last:
                e_out[k, tile] = energy
            elif late:
                e_tile[:, :, lanes] = energy.reshape(rows, SUBLANES, LANES)
            else:
                e_out[number, :, :, lanes] = energy.reshape(rows, SUBLANES, LANES)
            low_ref[:, lanes] = energy.astype(BF16)
            if own_copies and (k + 1) * LANES in (begin + BLOCK, bins):
                own_copies[begin // BLOCK].start()
        if not last:
            out_ref = o_out.at[:, tile]
        elif late:
            out_ref = o_tile
        else:
            out_ref = o_out.at[number]
        ocean_tile(
            dims, tile, (index, col_valid, got_col) if late or number == 0 else None,
            list(zip(row_valid, got_row)), parity,
            part_ref, grad_ref, mask_ref, w_ref, low_ref, drift_ref, out_ref,
        )
    if late and last:
        for copy in own_copies[-fields:]:
            copy.start()
        for copy in copies + own_copies:
            copy.wait()
    elif late:

        def pack(to_ref, take):
            for k in lane_chunks(bins):
                to_ref[..., k : k + LANES] = take(e_out.at[k // LANES])
            for q in range(fields):
                to_ref[..., bins + q * levels : bins + (q + 1) * levels] = take(o_out.at[q])

        for i, to_ref in enumerate(col_refs):
            tile, spots = column_place(dims, parity[0], i)
            pack(to_ref, lambda ref: ref[tile, spots, :])
        for i, to_ref in enumerate(row_refs):
            spots = row_place(dims, parity[1], i)
            pack(to_ref, lambda ref: ref[:, spots, :])


def swap_pairs(values, axis, other):
    size = {name: lax.axis_size(name) for name in (axis, other)}
    names = ("grp", "tile")

    def device(along, across):
        spot = {axis: along, other: across}
        return spot[names[0]] * lax.axis_size(names[1]) + spot[names[1]]

    got = []
    for index, value in enumerate(values):
        pairs = []
        for i in range(size[axis]):
            partner = i + 1 if (i - index) % 2 == 0 else i - 1
            for j in range(size[other]):
                if 0 <= partner < size[axis]:
                    pairs.append((device(i, j), device(partner, j)))
                elif j ^ 1 < size[other]:
                    pairs.append((device(i, j), device(i, j ^ 1)))
        got.append(lax.ppermute(value, names, pairs))
    return got


def local(spectrum, matrices, ownership, land_mask, courant, stokes_weight, ocean):
    bins, rows, cols = spectrum.shape
    fields, _, _, levels = ocean.shape
    mats = matrices.shape[2]
    tiles = cols // SUBLANES
    chunks = bins // LANES
    dims = (rows, cols, bins, levels, fields)
    n_col = 2
    n_row = 2 if lax.axis_size("tile") > 2 else 1
    e0 = jnp.transpose(spectrum, (1, 2, 0)).reshape(rows, tiles, SUBLANES, bins)
    o0 = ocean.reshape(fields, rows, tiles, SUBLANES, levels)
    m0 = matrices.reshape(mats, bins, bins)
    mask_t = land_mask.T
    owner_t = ownership.T
    counts = lax.axis_size("grp"), lax.axis_size("tile")

    vmem = pl.BlockSpec(memory_space=VMEM)
    hbm = pl.BlockSpec(memory_space=pltpu.HBM)

    def points(lead, width=LANES, dtype=F32):
        return VMEM((*lead, tiles, rows * SUBLANES, width), dtype)

    adv_shape = points((chunks,))
    o_shape = points((fields,), levels)
    window_shapes = [adv_shape, o_shape, points((2 * (fields - 2),), levels), points((2,))]
    wide = bins + fields * levels
    borders = [VMEM((rows, wide), F32)] * n_col + [VMEM((tiles, SUBLANES, wide), F32)] * n_row
    dma = pltpu.SemaphoreType.DMA

    def params(mib):
        return pltpu.CompilerParams(vmem_limit_bytes=mib * 2**20)

    def exchange(sent):
        return swap_pairs(sent[:n_col], "grp", "tile") + swap_pairs(sent[n_col:], "tile", "grp")

    sent = pl.pallas_call(
        functools.partial(first_kernel, dims, n_col, n_row),
        out_shape=borders
        + [VMEM((chunks, rows * cols, LANES), F32), VMEM((fields, rows * cols, levels), F32)],
        in_specs=[hbm, hbm],
        out_specs=[vmem] * (len(borders) + 2),
        scratch_shapes=[dma((chunks + 1,))],
        compiler_params=params(8),
        name="first",
    )(in_hbm(e0.reshape(-1, bins)), in_hbm(o0.reshape(fields, -1, levels)))
    e, o = sent[-2:]
    sent = sent[:-2]
    for step in range(STEPS):
        got = exchange(sent)
        if step == 0:
            adv, part, grad, flow, mask, owner, m, w = pl.pallas_call(
                functools.partial(window_kernel, dims, True),
                out_shape=window_shapes
                + [
                    points(()),
                    points((), LANES, jnp.int32),
                    VMEM(m0.shape, BF16),
                    VMEM(stokes_weight.shape, BF16),
                ],
                in_specs=[vmem] * 5 + [hbm] * 2,
                out_specs=[vmem] * 8,
                scratch_shapes=[dma((2,))],
                compiler_params=params(8),
                name="window_first",
            )(e, o, mask_t, owner_t, courant, in_hbm(m0), in_hbm(stokes_weight))
        else:
            adv, part, grad, flow = pl.pallas_call(
                functools.partial(window_kernel, dims, False),
                out_shape=window_shapes,
                in_specs=[vmem] * 4,
                out_specs=[vmem] * 4,
                compiler_params=params(8),
                name="window",
            )(e, o, mask, courant)
        last = step == STEPS - 1
        scratch = [VMEM((rows * SUBLANES, bins), BF16), VMEM((2, rows * SUBLANES, levels), F32)]
        if last:
            early_shape = [
                VMEM((tiles - 1, rows, SUBLANES, bins), F32),
                VMEM((tiles - 1, fields, rows * SUBLANES, levels), F32),
            ]
        else:
            early_shape = [adv_shape, o_shape]
        common = (mask, owner, m, w)
        adv, e, o = pl.pallas_call(
            functools.partial(step_kernel, dims, mats, counts, False, last, n_col, n_row),
            out_shape=[adv_shape] + early_shape,
            in_specs=[vmem] * (10 + n_row),
            out_specs=[vmem] * 3,
            scratch_shapes=scratch,
            input_output_aliases={1: 0},
            compiler_params=params(24),
            name="early_last" if last else "early",
        )(courant, adv, part, grad, flow, *common, got[0], *got[n_col:])
        e_at = 10 + n_row
        aliases = {1: 0}
        if last:
            late_shape = [pltpu.HBM(e0.shape, F32), pltpu.HBM(o0.shape, F32)]
            late_specs = [vmem, hbm, hbm]
            scratch += [
                VMEM((rows, SUBLANES, bins), F32),
                VMEM((fields, rows * SUBLANES, levels), F32),
                dma((tiles, fields + pl.cdiv(bins, BLOCK))),
            ]
        else:
            late_shape = early_shape + borders
            late_specs = [vmem] * (1 + len(late_shape))
            aliases.update({e_at: 1, e_at + 1: 2})
        _, e, o, *sent = pl.pallas_call(
            functools.partial(step_kernel, dims, mats, counts, True, last, n_col, n_row),
            out_shape=[adv_shape] + late_shape,
            in_specs=[vmem] * (12 + n_row),
            out_specs=late_specs,
            scratch_shapes=scratch,
            input_output_aliases=aliases,
            compiler_params=params(24),
            name="late_last" if last else "late",
        )(courant, adv, part, grad, flow, *common, got[1], *got[n_col:], e, o)
    energy = jnp.transpose(e.reshape(rows, cols, bins), (2, 0, 1))
    return energy, o.reshape(ocean.shape)


def solution(mesh):
    in_specs = (
        P(None, "tile", "grp"),
        P("tile", "grp", None, None, None),
        P("tile", "grp"),
        P("tile", "grp"),
        P(),
        P(),
        P(None, "tile", "grp", None),
    )
    out_specs = (P(None, "tile", "grp"), P(None, "tile", "grp", None))
    return jax.shard_map(local, mesh=mesh, in_specs=in_specs, out_specs=out_specs, check_vma=False)
```

```python
import functools

import jax
import jax.numpy as jnp
from jax import lax
from jax.experimental import pallas as pl
from jax.experimental.pallas import tpu as pltpu
from jax.sharding import PartitionSpec as P


STEPS = 2

current_gain = 0.2
source_gain = 0.5
mixing_side = 0.15
mixing_depth = 0.2
rotation = 0.3
transport = 0.5

LANES = 128
SUBLANES = 8
BLOCK = 512
VMEM = pltpu.VMEM
F32 = jnp.float32
BF16 = jnp.bfloat16


def in_hbm(x):
    return pltpu.with_memory_space_constraint(x, pltpu.HBM)


def lane_chunks(width):
    return range(0, width, LANES)


def low_side(parity, index):
    return parity if index == 0 else 1 - parity


def column_place(dims, parity, index):
    rows, cols, _, _, _ = dims
    high = 1 - low_side(parity, index)
    tile = high * (cols // SUBLANES - 1)
    return tile, pl.ds(high * (SUBLANES - 1), rows, stride=SUBLANES)


def row_place(dims, parity, index):
    high = 1 - low_side(parity, index)
    return pl.ds(pl.multiple_of(high * (dims[0] - 1) * SUBLANES, SUBLANES), SUBLANES)


def side_sign(parity, index):
    return jnp.where(low_side(parity, index) == 1, 1.0, -1.0).astype(F32)


def spot():
    return lax.axis_index("grp"), lax.axis_index("tile")


def parities():
    return tuple(lax.rem(i, 2) for i in spot())


def first_kernel(dims, n_col, n_row, e_hbm, o_hbm, *refs):
    rows, cols, bins, levels, fields = dims
    chunks = bins // LANES
    col_refs = refs[:n_col]
    row_refs = refs[n_col : n_col + n_row]
    e_ref, o_ref, sems = refs[n_col + n_row :]
    loads = [
        pltpu.make_async_copy(e_hbm.at[:, pl.ds(k * LANES, LANES)], e_ref.at[k], sems.at[k])
        for k in range(chunks)
    ]
    loads.append(pltpu.make_async_copy(o_hbm, o_ref, sems.at[chunks]))
    for copy in loads:
        copy.start()
    parity = parities()

    def pack(lanes, ref):
        for i, to_ref in enumerate(col_refs):
            high = 1 - low_side(parity[0], i)
            to_ref[:, lanes] = ref[pl.ds(high * (cols - 1), rows, stride=cols), :]
        for i, to_ref in enumerate(row_refs):
            high = 1 - low_side(parity[1], i)
            begin = pl.multiple_of(high * (rows - 1) * cols, cols)
            to_ref[:, :, lanes] = ref[pl.ds(begin, cols), :].reshape(-1, SUBLANES, LANES)

    for k in range(chunks):
        loads[k].wait()
        pack(slice(k * LANES, (k + 1) * LANES), e_ref.at[k])
    loads[chunks].wait()
    for q in range(fields):
        pack(slice(bins + q * levels, bins + (q + 1) * levels), o_ref.at[q])


def shifted(parts, axis_ids, ahead):
    first, final = axis_ids
    out = []
    if ahead:
        turned = [pltpu.roll(x, SUBLANES - 1, axis=0) for x in parts]
        for i, x in enumerate(turned):
            out.append(jnp.where(final, turned[i + 1] if i + 1 < len(parts) else 0.0, x))
    else:
        turned = [pltpu.roll(x, 1, axis=0) for x in parts]
        for i, x in enumerate(turned):
            out.append(jnp.where(first, turned[i - 1] if i else 0.0, x))
    return out


def sublane_ends():
    ids = lax.broadcasted_iota(jnp.int32, (SUBLANES, LANES), 0)
    return ids == 0, ids == SUBLANES - 1


def span(r):
    return slice(r * SUBLANES, (r + 1) * SUBLANES)


def advect_all(dims, energy_at, flow_ref, courant_ref, adv_ref):
    rows, cols, bins, _, _ = dims
    ends = sublane_ends()
    tiles = cols // SUBLANES

    def body(k, _):
        lanes = pl.ds(pl.multiple_of(k * LANES, LANES), LANES)
        speeds = [
            jnp.broadcast_to(courant_ref[way : way + 1, lanes], (SUBLANES, LANES))
            for way in range(2)
        ]

        def load(r):
            if r >= rows:
                return None
            return [energy_at(k, i, r) for i in range(tiles)]

        mid = load(0)
        falls = mid
        for r in range(rows):
            following = load(r + 1)
            if following is None:
                falls_next = [-x for x in mid]
            else:
                falls_next = [b - a for a, b in zip(mid, following)]
            west = shifted(mid, ends, False)
            east = shifted(mid, ends, True)
            for i in range(tiles):
                speed_x = speeds[0] + flow_ref[0, i, span(r), :]
                speed_y = speeds[1] + flow_ref[1, i, span(r), :]
                flux = speed_x * jnp.where(speed_x > 0, mid[i] - west[i], east[i] - mid[i])
                flux = flux + speed_y * jnp.where(speed_y > 0, falls[i], falls_next[i])
                adv_ref[k, i, span(r), :] = mid[i] - flux
            mid, falls = following, falls_next
        return 0

    lax.fori_loop(0, bins // LANES, body, 0)


def ocean_all(dims, ocean_at, mask_ref, part_ref, grad_ref):
    rows, cols, _, levels, fields = dims
    ends = sublane_ends()
    level_id = lax.broadcasted_iota(jnp.int32, (SUBLANES, levels), 1)
    top = level_id == 0
    bottom = level_id == levels - 1
    tiles = cols // SUBLANES

    for q in range(fields):
        north = None
        mid = [ocean_at(q, i, 0) for i in range(tiles)]
        for r in range(rows):
            south = None
            if r + 1 < rows:
                south = [ocean_at(q, i, r + 1) for i in range(tiles)]
            west = shifted(mid, ends, False)
            east = shifted(mid, ends, True)
            for i in range(tiles):
                own = mid[i]
                if north is None:
                    across, slope = south[i], south[i]
                elif south is None:
                    across, slope = north[i], -north[i]
                else:
                    across, slope = north[i] + south[i], south[i] - north[i]
                above = jnp.where(top, 0.0, pltpu.roll(own, 1, axis=1))
                below = jnp.where(bottom, 0.0, pltpu.roll(own, levels - 1, axis=1))
                tend = mixing_side * (across + (west[i] + east[i])) + mixing_depth * (above + below)
                tend = tend - (4 * mixing_side + 2 * mixing_depth) * own
                if q == 0:
                    tend = tend + rotation * ocean_at(1, i, r)
                elif q == 1:
                    tend = tend - rotation * ocean_at(0, i, r)
                else:
                    grad_ref[2 * (q - 2), i, span(r), :] = east[i] - west[i]
                    grad_ref[2 * (q - 2) + 1, i, span(r), :] = slope
                part_ref[q, i, span(r), :] = own + mask_ref[i, span(r), :] * tend
            north, mid = mid, south


def window_kernel(dims, first, e_ref, o_ref, *refs):
    rows, cols, _, _, _ = dims
    tiles = cols // SUBLANES
    if first:
        mask_t, owner_t, courant_ref, m_hbm, w_hbm, adv_ref, part_ref, grad_ref, flow_ref = refs[:9]
        mask_ref, owner_ref, m_ref, w_ref, sems = refs[9:]
        copies = [
            pltpu.make_async_copy(m_hbm, m_ref, sems.at[0]),
            pltpu.make_async_copy(w_hbm, w_ref, sems.at[1]),
        ]
        for copy in copies:
            copy.start()
        mask = mask_t[...].astype(F32)
        owner = jnp.where(mask_t[...] == 1, owner_t[...], -1)
        for i in range(tiles):
            for r in range(rows):
                for to_ref, values in ((mask_ref, mask), (owner_ref, owner)):
                    to_ref[i, span(r), :] = jnp.broadcast_to(
                        values[span(i), r : r + 1], (SUBLANES, LANES)
                    )
    else:
        mask_ref, courant_ref, adv_ref, part_ref, grad_ref, flow_ref = refs
        copies = []

    def energy_at(k, i, r):
        return e_ref[k, span(r * tiles + i), :] if first else e_ref[k, i, span(r), :]

    def ocean_at(q, i, r):
        return o_ref[q, span(r * tiles + i), :] if first else o_ref[q, i, span(r), :]

    for way in range(2):
        for i in range(tiles):
            for r in range(rows):
                flow_ref[way, i, span(r), :] = jnp.broadcast_to(
                    current_gain * ocean_at(way, i, r)[:, 0:1], (SUBLANES, LANES)
                )
    ocean_all(dims, ocean_at, mask_ref, part_ref, grad_ref)
    advect_all(dims, energy_at, flow_ref, courant_ref, adv_ref)
    for copy in copies:
        copy.wait()


def real(spot, index):
    place, count = spot
    if index == 0 and count % 2 == 0:
        return None
    low = low_side(lax.rem(place, 2), index)
    partner = place + 1 - 2 * low
    return jnp.logical_and(partner >= 0, partner < count)


def kept(valid, value):
    return value if valid is None else jnp.where(valid, value, 0.0)


def fix_column(dims, parity, index, valid, halo_ref, flow_ref, courant_ref, adv_ref):
    tile, spots = column_place(dims, parity, index)
    sign = side_sign(parity, index)
    speed = flow_ref[0, tile, spots, :]
    for k in range(dims[2] // LANES):
        lanes = slice(k * LANES, (k + 1) * LANES)
        inward = jnp.maximum(sign * (courant_ref[0:1, lanes] + speed), 0.0)
        adv_ref[k, tile, spots, :] = (
            adv_ref[k, tile, spots, :] + inward * kept(valid, halo_ref[:, lanes])
        )


def fix_row(dims, parity, index, valid, halo_ref, flow_ref, courant_ref, adv_ref):
    spots = row_place(dims, parity, index)
    sign = side_sign(parity, index)
    for i in range(dims[1] // SUBLANES):
        speed = flow_ref[1, i, spots, :]
        for k in range(dims[2] // LANES):
            lanes = slice(k * LANES, (k + 1) * LANES)
            inward = jnp.maximum(sign * (courant_ref[1:2, lanes] + speed), 0.0)
            adv_ref[k, i, spots, :] = (
                adv_ref[k, i, spots, :] + inward * kept(valid, halo_ref[i, :, lanes])
            )


def ocean_border(dims, sign, along, tile, spots, halo, mask_ref, drift_ref, out_ref):
    _, _, bins, levels, fields = dims
    sea = mask_ref[tile, spots, :]
    shear = (sign * (0.5 * transport)) * drift_ref[along, spots, :]
    for q in range(fields):
        value = halo(slice(bins + q * levels, bins + (q + 1) * levels))
        gain = mixing_side if q < 2 else mixing_side + shear
        out_ref[q, spots, :] = out_ref[q, spots, :] + sea * (gain * value)


def low_of(dims, mats, tile, adv_ref, owner_ref):
    owner = owner_ref[tile]
    return jnp.concatenate(
        [
            jnp.where(owner == m, adv_ref[k, tile], 0.0).astype(BF16)
            for m in range(mats)
            for k in range(dims[2] // LANES)
        ],
        axis=1,
    )


def source_of(mats, low, m_ref, begin, end):
    weights = jnp.concatenate([m_ref[m, begin:end, :] for m in range(mats)], axis=1)
    return lax.dot_general(low, weights, (((1,), (1,)), ((), ())), preferred_element_type=F32)


def ocean_tile(dims, tile, col_border, row_borders, parity, part_ref, grad_ref, mask_ref,
               w_ref, low_ref, drift_ref, out_ref):
    _, _, _, levels, fields = dims
    drift = jnp.dot(low_ref[...], w_ref[...], preferred_element_type=F32)
    for k in range(2):
        drift_ref[k] = drift[:, k * levels : (k + 1) * levels]
    sea = mask_ref[tile]
    along = sea * drift[:, 0:levels]
    across = sea * drift[:, levels : 2 * levels]
    out_ref[0] = part_ref[0, tile] + rotation * across
    out_ref[1] = part_ref[1, tile] - rotation * along
    for q in range(2, fields):
        grad = along * grad_ref[2 * (q - 2), tile] + across * grad_ref[2 * (q - 2) + 1, tile]
        out_ref[q] = part_ref[q, tile] - (0.5 * transport) * grad
    if col_border is not None:
        index, valid, col_ref = col_border
        _, spots = column_place(dims, parity[0], index)
        ocean_border(
            dims, side_sign(parity[0], index), 0, tile, spots,
            lambda lanes: kept(valid, col_ref[:, lanes]), mask_ref, drift_ref, out_ref,
        )
    for index, (valid, row_ref) in enumerate(row_borders):
        ocean_border(
            dims, side_sign(parity[1], index), 1, tile, row_place(dims, parity[1], index),
            lambda lanes: kept(valid, row_ref[tile, :, lanes]), mask_ref, drift_ref, out_ref,
        )


def step_kernel(dims, mats, counts, late, last, n_col, n_row, *refs):
    rows, cols, bins, levels, fields = dims
    tiles = cols // SUBLANES
    courant_ref, _, part_ref, grad_ref, flow_ref = refs[:5]
    mask_ref, owner_ref, m_ref, w_ref = refs[5:9]
    refs = refs[9:]
    got_col, got_row, refs = refs[0], refs[1 : 1 + n_row], refs[1 + n_row :]
    if late:
        e_early, o_early, *refs = refs
    adv_ref, e_out, o_out, *refs = refs
    if late and not last:
        col_refs, row_refs, refs = refs[:n_col], refs[n_col : n_col + n_row], refs[n_col + n_row :]
    low_ref, drift_ref, *refs = refs
    here, parity = spot(), parities()
    index = 1 if late else 0
    col_valid = real((here[0], counts[0]), index)
    row_valid = [real((here[1], counts[1]), i) for i in range(n_row)]
    walk = parity[0]
    todo = [walk * i + (1 - walk) * (tiles - 1 - i) for i in range(tiles)]
    copies = []
    if late and last:
        e_tile, o_tile, sems = refs

        def store(number, e_from, o_from):
            tile = todo[number]
            made = []
            for begin in range(0, bins, BLOCK):
                lanes = pl.ds(begin, min(BLOCK, bins - begin))
                made.append(
                    pltpu.make_async_copy(
                        e_from.at[:, :, lanes],
                        e_out.at[:, tile, :, lanes],
                        sems.at[number, fields + begin // BLOCK],
                    )
                )
            for q in range(fields):
                made.append(
                    pltpu.make_async_copy(
                        o_from.at[q].reshape(rows, SUBLANES, levels),
                        o_out.at[q, :, tile],
                        sems.at[number, q],
                    )
                )
            return made

        for number in range(tiles - 1):
            copies += store(number, e_early.at[number], o_early.at[number])
        for copy in copies:
            copy.start()
    fixed = (flow_ref, courant_ref, adv_ref)
    if not late:
        for row_index in range(n_row):
            fix_row(
                dims, parity[1], row_index, row_valid[row_index], got_row[row_index], *fixed
            )
    fix_column(dims, parity[0], index, col_valid, got_col, *fixed)
    for number, tile in enumerate(todo):
        if late != (number == tiles - 1):
            continue
        low = low_of(dims, mats, tile, adv_ref, owner_ref)
        sea = mask_ref[tile]
        own_copies = store(number, e_tile, o_tile) if late and last else None
        for k in range(bins // LANES):
            lanes = slice(k * LANES, (k + 1) * LANES)
            begin = k * LANES // BLOCK * BLOCK
            if k * LANES == begin:
                source = source_of(mats, low, m_ref, begin, min(begin + BLOCK, bins))
            gain = source[:, k * LANES - begin : (k + 1) * LANES - begin]
            energy = sea * (adv_ref[k, tile] + source_gain * gain)
            if not last:
                e_out[k, tile] = energy
            elif late:
                e_tile[:, :, lanes] = energy.reshape(rows, SUBLANES, LANES)
            else:
                e_out[number, :, :, lanes] = energy.reshape(rows, SUBLANES, LANES)
            low_ref[:, lanes] = energy.astype(BF16)
            if own_copies and (k + 1) * LANES in (begin + BLOCK, bins):
                own_copies[begin // BLOCK].start()
        if not last:
            out_ref = o_out.at[:, tile]
        elif late:
            out_ref = o_tile
        else:
            out_ref = o_out.at[number]
        ocean_tile(
            dims, tile, (index, col_valid, got_col) if late or number == 0 else None,
            list(zip(row_valid, got_row)), parity,
            part_ref, grad_ref, mask_ref, w_ref, low_ref, drift_ref, out_ref,
        )
    if late and last:
        for copy in own_copies[-fields:]:
            copy.start()
        for copy in copies + own_copies:
            copy.wait()
    elif late:

        def pack(to_ref, take):
            for k in lane_chunks(bins):
                to_ref[..., k : k + LANES] = take(e_out.at[k // LANES])
            for q in range(fields):
                to_ref[..., bins + q * levels : bins + (q + 1) * levels] = take(o_out.at[q])

        for i, to_ref in enumerate(col_refs):
            tile, spots = column_place(dims, parity[0], i)
            pack(to_ref, lambda ref: ref[tile, spots, :])
        for i, to_ref in enumerate(row_refs):
            spots = row_place(dims, parity[1], i)
            pack(to_ref, lambda ref: ref[:, spots, :])


def swap_pairs(values, axis, other):
    size = {name: lax.axis_size(name) for name in (axis, other)}
    names = ("grp", "tile")

    def device(along, across):
        spot = {axis: along, other: across}
        return spot[names[0]] * lax.axis_size(names[1]) + spot[names[1]]

    got = []
    for index, value in enumerate(values):
        pairs = []
        for i in range(size[axis]):
            partner = i + 1 if (i - index) % 2 == 0 else i - 1
            for j in range(size[other]):
                if 0 <= partner < size[axis]:
                    pairs.append((device(i, j), device(partner, j)))
                elif j ^ 1 < size[other]:
                    pairs.append((device(i, j), device(i, j ^ 1)))
        got.append(lax.ppermute(value, names, pairs))
    return got


def local(spectrum, matrices, ownership, land_mask, courant, stokes_weight, ocean):
    bins, rows, cols = spectrum.shape
    fields, _, _, levels = ocean.shape
    mats = matrices.shape[2]
    tiles = cols // SUBLANES
    chunks = bins // LANES
    dims = (rows, cols, bins, levels, fields)
    n_col = 2
    n_row = 2 if lax.axis_size("tile") > 2 else 1
    e0 = jnp.transpose(spectrum, (1, 2, 0)).reshape(rows, tiles, SUBLANES, bins)
    o0 = ocean.reshape(fields, rows, tiles, SUBLANES, levels)
    m0 = matrices.reshape(mats, bins, bins)
    mask_t = land_mask.T
    owner_t = ownership.T
    counts = lax.axis_size("grp"), lax.axis_size("tile")

    vmem = pl.BlockSpec(memory_space=VMEM)
    hbm = pl.BlockSpec(memory_space=pltpu.HBM)

    def points(lead, width=LANES, dtype=F32):
        return VMEM((*lead, tiles, rows * SUBLANES, width), dtype)

    adv_shape = points((chunks,))
    o_shape = points((fields,), levels)
    window_shapes = [adv_shape, o_shape, points((2 * (fields - 2),), levels), points((2,))]
    wide = bins + fields * levels
    borders = [VMEM((rows, wide), F32)] * n_col + [VMEM((tiles, SUBLANES, wide), F32)] * n_row
    dma = pltpu.SemaphoreType.DMA

    def params(mib):
        return pltpu.CompilerParams(vmem_limit_bytes=mib * 2**20)

    def exchange(sent):
        return swap_pairs(sent[:n_col], "grp", "tile") + swap_pairs(sent[n_col:], "tile", "grp")

    sent = pl.pallas_call(
        functools.partial(first_kernel, dims, n_col, n_row),
        out_shape=borders
        + [VMEM((chunks, rows * cols, LANES), F32), VMEM((fields, rows * cols, levels), F32)],
        in_specs=[hbm, hbm],
        out_specs=[vmem] * (len(borders) + 2),
        scratch_shapes=[dma((chunks + 1,))],
        compiler_params=params(8),
        name="first",
    )(in_hbm(e0.reshape(-1, bins)), in_hbm(o0.reshape(fields, -1, levels)))
    e, o = sent[-2:]
    sent = sent[:-2]
    for step in range(STEPS):
        got = exchange(sent)
        if step == 0:
            adv, part, grad, flow, mask, owner, m, w = pl.pallas_call(
                functools.partial(window_kernel, dims, True),
                out_shape=window_shapes
                + [
                    points(()),
                    points((), LANES, jnp.int32),
                    VMEM(m0.shape, BF16),
                    VMEM(stokes_weight.shape, BF16),
                ],
                in_specs=[vmem] * 5 + [hbm] * 2,
                out_specs=[vmem] * 8,
                scratch_shapes=[dma((2,))],
                compiler_params=params(8),
                name="window_first",
            )(e, o, mask_t, owner_t, courant, in_hbm(m0), in_hbm(stokes_weight))
        else:
            adv, part, grad, flow = pl.pallas_call(
                functools.partial(window_kernel, dims, False),
                out_shape=window_shapes,
                in_specs=[vmem] * 4,
                out_specs=[vmem] * 4,
                compiler_params=params(8),
                name="window",
            )(e, o, mask, courant)
        last = step == STEPS - 1
        scratch = [VMEM((rows * SUBLANES, bins), BF16), VMEM((2, rows * SUBLANES, levels), F32)]
        if last:
            early_shape = [
                VMEM((tiles - 1, rows, SUBLANES, bins), F32),
                VMEM((tiles - 1, fields, rows * SUBLANES, levels), F32),
            ]
        else:
            early_shape = [adv_shape, o_shape]
        common = (mask, owner, m, w)
        adv, e, o = pl.pallas_call(
            functools.partial(step_kernel, dims, mats, counts, False, last, n_col, n_row),
            out_shape=[adv_shape] + early_shape,
            in_specs=[vmem] * (10 + n_row),
            out_specs=[vmem] * 3,
            scratch_shapes=scratch,
            input_output_aliases={1: 0},
            compiler_params=params(24),
            name="early_last" if last else "early",
        )(courant, adv, part, grad, flow, *common, got[0], *got[n_col:])
        e_at = 10 + n_row
        aliases = {1: 0}
        if last:
            late_shape = [pltpu.HBM(e0.shape, F32), pltpu.HBM(o0.shape, F32)]
            late_specs = [vmem, hbm, hbm]
            scratch += [
                VMEM((rows, SUBLANES, bins), F32),
                VMEM((fields, rows * SUBLANES, levels), F32),
                dma((tiles, fields + pl.cdiv(bins, BLOCK))),
            ]
        else:
            late_shape = early_shape + borders
            late_specs = [vmem] * (1 + len(late_shape))
            aliases.update({e_at: 1, e_at + 1: 2})
        _, e, o, *sent = pl.pallas_call(
            functools.partial(step_kernel, dims, mats, counts, True, last, n_col, n_row),
            out_shape=[adv_shape] + late_shape,
            in_specs=[vmem] * (12 + n_row),
            out_specs=late_specs,
            scratch_shapes=scratch,
            input_output_aliases=aliases,
            compiler_params=params(24),
            name="late_last" if last else "late",
        )(courant, adv, part, grad, flow, *common, got[1], *got[n_col:], e, o)
    energy = jnp.transpose(e.reshape(rows, cols, bins), (2, 0, 1))
    return energy, o.reshape(ocean.shape)


def solution(mesh):
    in_specs = (
        P(None, "tile", "grp"),
        P("tile", "grp", None, None, None),
        P("tile", "grp"),
        P("tile", "grp"),
        P(),
        P(),
        P(None, "tile", "grp", None),
    )
    out_specs = (P(None, "tile", "grp"), P(None, "tile", "grp", None))
    return jax.shard_map(local, mesh=mesh, in_specs=in_specs, out_specs=out_specs, check_vma=False)
```
